32 devices in a mesh: blk: 8 (over z, x), head: 4 (over y, core).
Axes of the slice: x: 2, y: 2, z: 4, core: 2. Of those that a mesh axis runs over, the one named last changes fastest.
Arguments:
- queries: bfloat16 [4096, 1024], P(('blk', 'head')), may hold values from -6 to 6
- key_vectors: bfloat16 [4096, 1024], P(('blk', 'head')), may hold values from -6 to 6
- value_vectors: bfloat16 [4096, 1024], P(('blk', 'head')), may hold values from -6 to 6
- grad_output: bfloat16 [4096, 1024], P(('blk', 'head')), may hold values from -6 to 6
- lengths: int32 [4], replicated, may hold values from 1 to 2048, 4096 in all
Outputs:
- grad_queries: bfloat16 [4096, 1024], P(('blk', 'head'))
- grad_keys: bfloat16 [4096, 1024], P(('blk', 'head'))
- grad_values: bfloat16 [4096, 1024], P(('blk', 'head'))
The draws below stay inside these ranges and needn't reach their ends.
Inputs may be any that keep to these rules, and one draw needn't show every extreme that they name: 4 positive lengths that sum to 4096; the longest is exactly 2048.
All inputs are finite; a program needn't handle non-finite values.
Results may differ from the reference program's by a relative error of at most 0.0086.
Values may be sent and summed in bfloat16 or wider, within the bound.
No kernel may reach another device: no remote copies, remote signals or barrier semaphores. Data moves between devices by JAX's collectives and lax.ppermute only.
A program may use at most 64 MiB of HBM per device.

```python
import math
import jax
import jax.numpy as jnp
import numpy as np
from jax import lax

HEADS = 16
DH = 64
WIN = 64
NREC = 4
FRAMES = 4096
RECMAX = 2048


def row_scales(key):
    return jnp.exp(jax.random.uniform(key, (FRAMES, 1), jnp.float32, math.log(0.5), math.log(2.0)))


def draw_side(key, salt):
    noise_key, scale_key = jax.random.split(jax.random.fold_in(key, salt))
    scales = row_scales(scale_key)
    columns = HEADS * DH
    result = jax.random.normal(noise_key, (FRAMES, columns), jnp.float32) * scales
    return jnp.clip(result, -6.0, 6.0).astype(jnp.bfloat16)


def draw_queries(key, part):
    return draw_side(key, 1)


def draw_key_vectors(key, part):
    return draw_side(key, 2)


def block_levels(own_key, extent, shards, smallest, largest):
    factor_of, own = 1.0, jax.random.fold_in(own_key, 6)
    for dim, shards_of in shards:
        steps = jnp.exp(jax.random.uniform(jax.random.fold_in(own, dim), (shards_of,), jnp.float32, smallest / len(shards), largest / len(shards)))
        factor_of = factor_of * jnp.repeat(steps, extent[dim] // shards_of).reshape([-1 if axis == dim else 1 for axis in range(len(extent))])
    return factor_of


def length_profile(count, total, reach, slope):
    weights = [(1 << 20) // math.isqrt(standing ** slope) + 1 for standing in range(2, count + 1)]
    rest, holding = total - reach - (count - 1), [1] * (count - 1)
    while rest > 0:
        movable = [i for i in range(count - 1) if holding[i] < reach]
        whole, remaining = sum([weights[i] for i in movable]), rest
        for i in movable:
            addition = min(reach - holding[i], max(1, remaining * weights[i] // whole), rest)
            holding[i] = holding[i] + addition
            rest = rest - addition
    return np.array([reach] + holding)


def uneven_parts(own_key, count, total, bound, lean):
    if count == 2:
        one = jax.random.randint(own_key, (), max(1, total - bound), min(bound, total - 1) + 1)
        return jnp.stack([one, total - one])
    sizes = jnp.asarray(length_profile(count, total, bound, lean), jnp.int32)
    pairs = (count - 1) // 2
    source_of, taker = sizes[1:1 + 2 * pairs:2], sizes[2:2 + 2 * pairs:2]
    room = jnp.minimum(source_of - 1, bound - taker)
    passed = jax.random.randint(jax.random.fold_in(own_key, 1), (pairs,), 0, 1 << 20) % (room + 1)
    sizes = sizes.at[1:1 + 2 * pairs:2].set(source_of - passed).at[2:2 + 2 * pairs:2].set(taker + passed)
    return sizes[jax.random.permutation(jax.random.fold_in(own_key, 2), count)]


def scatter_about(stream_key, dims, scale, bound, shards=(), kind=jnp.bfloat16):
    factor_of = block_levels(stream_key, dims, shards, -0.22, 0.18) if shards else 1.0
    values = jax.random.normal(stream_key, dims, jnp.float32) * scale * factor_of
    return jnp.minimum(jnp.maximum(values, -bound), bound).astype(kind)


def setup_inputs(seed: int = 0) -> dict:
    keys = jax.random.split(jax.random.key(seed), 6)
    queries = draw_queries(jax.random.fold_in(keys[5], 71), 0)
    key_vectors = draw_key_vectors(jax.random.fold_in(keys[5], 71), 0)
    value_vectors = scatter_about(keys[2], (FRAMES, HEADS * DH), 1.0, 6.0, ((0, 32),))
    grad_output = scatter_about(keys[3], (FRAMES, HEADS * DH), 1.0, 6.0, ((0, 32),))
    lengths = uneven_parts(keys[4], NREC, FRAMES, RECMAX, 2).astype(jnp.int32)
    return dict(queries=queries, key_vectors=key_vectors, value_vectors=value_vectors, grad_output=grad_output, lengths=lengths)


def recording_of(positions, rec_ends):
    return lax.optimization_barrier(jnp.sum((rec_ends[None, :] <= positions[:, None]).astype(jnp.int32), axis=1))

def pad_rows(array):
    return jnp.pad(array.astype(jnp.float32), ((WIN, WIN), (0, 0)))

def reference(queries, key_vectors, value_vectors, grad_output, lengths):
    frames = queries.shape[0]
    columns = queries.shape[1]
    head_count = columns // DH
    rec_ends = jnp.cumsum(lengths).astype(jnp.int32)
    step_rows = math.gcd(512, frames)
    key_span = step_rows + 2 * WIN
    score_scale = 1.0 / math.sqrt(DH)
    padded_keys = pad_rows(key_vectors)
    padded_values = pad_rows(value_vectors)

    def block_step(state_pair, block_index):
        key_acc, value_acc = state_pair
        offset = (block_index * step_rows).astype(jnp.int32)
        query_block = lax.dynamic_slice_in_dim(queries, offset, step_rows, 0).astype(jnp.float32).reshape(step_rows, head_count, DH)
        grad_block = lax.dynamic_slice_in_dim(grad_output, offset, step_rows, 0).astype(jnp.float32).reshape(step_rows, head_count, DH)
        key_block = lax.dynamic_slice_in_dim(padded_keys, offset, key_span, 0).reshape(key_span, head_count, DH)
        value_block = lax.dynamic_slice_in_dim(padded_values, offset, key_span, 0).reshape(key_span, head_count, DH)
        query_pos = offset + jnp.arange(step_rows, dtype=jnp.int32)
        key_pos = offset - WIN + jnp.arange(key_span, dtype=jnp.int32)
        inside = (key_pos >= 0) & (key_pos < frames)
        visible = jnp.abs(query_pos[:, None] - key_pos[None, :]) <= WIN
        visible = visible & (recording_of(query_pos, rec_ends)[:, None] == recording_of(key_pos, rec_ends)[None, :])
        visible = visible & (inside[None, :] | (query_pos[:, None] == key_pos[None, :]))
        scores = jnp.einsum('qhd,khd->hqk', query_block, key_block) * score_scale
        scores = jnp.where(visible[None], scores, -1e+30)
        row_max = lax.optimization_barrier(jnp.max(scores, axis=-1, keepdims=True))
        weights = jnp.where(visible[None], jnp.exp(scores - row_max), 0.0)
        probs = weights / lax.optimization_barrier(jnp.sum(weights, axis=-1, keepdims=True))
        probs_low = lax.optimization_barrier(probs.astype(jnp.bfloat16)).astype(jnp.float32)
        value_part = jnp.einsum('hqk,qhd->khd', probs_low, grad_block)
        prob_grad = jnp.einsum('qhd,khd->hqk', grad_block, value_block)
        row_delta = lax.optimization_barrier(jnp.sum(probs * prob_grad, axis=-1, keepdims=True))
        score_grad = (probs * (prob_grad - row_delta) * score_scale).astype(jnp.bfloat16)
        score_grad = lax.optimization_barrier(score_grad).astype(jnp.float32)
        query_grad = jnp.einsum('hqk,khd->qhd', score_grad, key_block).reshape(step_rows, columns)
        key_part = jnp.einsum('hqk,qhd->khd', score_grad, query_block).reshape(key_span, columns)
        key_acc = lax.dynamic_update_slice_in_dim(key_acc, lax.dynamic_slice_in_dim(key_acc, offset, key_span, 0) + key_part, offset, 0)
        value_acc = lax.dynamic_update_slice_in_dim(value_acc, lax.dynamic_slice_in_dim(value_acc, offset, key_span, 0) + value_part.reshape(key_span, columns), offset, 0)
        return ((key_acc, value_acc), query_grad.astype(jnp.bfloat16))
    zeros_acc = jnp.zeros((frames + 2 * WIN, columns), jnp.float32)
    final_pair, query_blocks = lax.scan(block_step, (zeros_acc, zeros_acc), jnp.arange(frames // step_rows, dtype=jnp.int32))
    grad_queries = query_blocks.reshape(frames, columns)
    grad_keys = final_pair[0][WIN:WIN + frames].astype(jnp.bfloat16)
    grad_values = final_pair[1][WIN:WIN + frames].astype(jnp.bfloat16)
    return (grad_queries, grad_keys, grad_values)
```

```python
import functools

import jax
import jax.numpy as jnp
from jax import lax
from jax.experimental import pallas as pl
from jax.experimental.pallas import tpu as pltpu
from jax.sharding import PartitionSpec as P

DH = 64
WIN = 64
PAIR = 2 * DH
SCALE = DH ** (-0.5)
NEG = -1e30
AXES = ("blk", "head")
F32 = jnp.float32
BF16 = jnp.bfloat16


def flat_index():
    return lax.axis_index("blk") * lax.axis_size("head") + lax.axis_index("head")


def recording_of(pos, len_ref):
    rec = jnp.where(pos < 0, -1, 0)
    end = jnp.int32(0)
    for r in range(len_ref.shape[0]):
        end = end + len_ref[r]
        rec = rec + jnp.where(pos >= end, 1, 0)
    return rec


def bias_of(key_first, query_first, keys, queries, lane_queries, len_ref):
    kpos = key_first + lax.broadcasted_iota(jnp.int32, (keys, queries), 0)
    qpos = query_first + lax.broadcasted_iota(jnp.int32, (keys, queries), 1) % lane_queries
    near = jnp.abs(kpos - qpos) <= WIN
    same = recording_of(kpos, len_ref) == recording_of(qpos, len_ref)
    return jnp.where(near & same, 0.0, NEG).astype(F32)


def split_heads(pair):
    lane = lax.broadcasted_iota(jnp.int32, pair.shape, 1)
    zero = jnp.zeros_like(pair)
    return jnp.concatenate([jnp.where(lane < DH, pair, zero), jnp.where(lane < DH, zero, pair)], axis=0)


def nt(a, b):
    return lax.dot_general(a, b, (((1,), (1,)), ((), ())), preferred_element_type=F32)


def nn(a, b):
    return lax.dot_general(a, b, (((1,), (0,)), ((), ())), preferred_element_type=F32)


def tn(a, b):
    return lax.dot_general(a, b, (((0,), (0,)), ((), ())), preferred_element_type=F32)


def local_kernel(len_ref, q_ref, k_ref, v_ref, g_ref, qg_o, st_o, qg_e, st_e):
    rows, cols = q_ref.shape
    me = flat_index()
    odd = lax.rem(me, 2)
    base = me * rows
    half = rows // 2
    for out, first in ((qg_o, odd * half), (qg_e, (1 - odd) * half)):
        first = pl.multiple_of(first, half)
        out[:half, :] = q_ref[pl.ds(first, half), :]
        out[half:, :] = g_ref[pl.ds(first, half), :]
    bias = bias_of(base, base, rows, rows, rows, len_ref)
    bias = jnp.concatenate([bias, bias], axis=1)
    lane = lax.broadcasted_iota(jnp.int32, (1, rows), 1)
    for p in range(cols // PAIR):
        cs = slice(p * PAIR, (p + 1) * PAIR)
        qq = split_heads(q_ref[:, cs]) * BF16(SCALE)
        gg = split_heads(g_ref[:, cs])
        s = nt(k_ref[:, cs], qq) + bias
        dp = nt(v_ref[:, cs], gg)
        m = jnp.max(s, axis=0, keepdims=True)
        e = jnp.exp(s - m)
        l = jnp.sum(e, axis=0, keepdims=True)
        d = jnp.sum(e * dp, axis=0, keepdims=True)
        for n, stat in enumerate((m, l, d)):
            a, b = stat[:, :rows], stat[:, rows:]
            lo = jnp.where(lane < half, a, pltpu.roll(b, half, 1))
            hi = jnp.where(lane < half, pltpu.roll(a, half, 1), b)
            r = 3 * p + n
            st_o[r : r + 1, :] = jnp.where(odd == 1, hi, lo)
            st_e[r : r + 1, :] = jnp.where(odd == 1, lo, hi)


def own_kernel(len_ref, q_ref, k_ref, v_ref, g_ref, kv_o, kv_e, dq_ref, dk_ref, dv_ref, kx, vx):
    rows, cols = q_ref.shape
    me = flat_index()
    odd = lax.rem(me, 2)
    base = me * rows
    half = rows // 2
    for dst, own, o in ((kx, k_ref, 0), (vx, v_ref, half)):
        dst[half : half + rows, :] = own[...]

        @pl.when(odd == 1)
        def _():
            dst[:half, :] = kv_e[o : o + half, :]
            dst[half + rows :, :] = kv_o[o : o + half, :]

        @pl.when(odd == 0)
        def _():
            dst[:half, :] = kv_o[o : o + half, :]
            dst[half + rows :, :] = kv_e[o : o + half, :]

    span = rows + 2 * half
    bias = bias_of(base - half, base, span, rows, rows, len_ref)
    bias = jnp.concatenate([bias, bias], axis=1)
    lane = lax.broadcasted_iota(jnp.int32, (rows, PAIR), 1)
    for p in range(cols // PAIR):
        cs = slice(p * PAIR, (p + 1) * PAIR)
        qq = split_heads(q_ref[:, cs]) * BF16(SCALE)
        gg = split_heads(g_ref[:, cs])
        kp = kx[:, cs]
        s = nt(kp, qq) + bias
        dp = nt(vx[:, cs], gg)
        m = jnp.max(s, axis=0, keepdims=True)
        e = jnp.exp(s - m)
        inv = 1.0 / jnp.sum(e, axis=0, keepdims=True)
        prob = e * inv
        delta = jnp.sum(prob * dp, axis=0, keepdims=True)
        ds = (prob * (dp - delta)).astype(BF16)
        dv_ref[:, cs] = nn(prob[half : half + rows].astype(BF16), gg)
        dk_ref[:, cs] = nn(ds[half : half + rows], qq)
        dq2 = tn(ds, kp)
        dq_ref[:, cs] = (jnp.where(lane < DH, dq2[:rows], dq2[rows:]) * SCALE).astype(BF16)


def edge_kernel(len_ref, k_ref, v_ref, qg_o, st_o, qg_e, st_e, dka_ref, dva_ref, dk_ref, dv_ref, qg, st):
    rows, cols = k_ref.shape
    me = flat_index()
    odd = lax.rem(me, 2)
    base = me * rows
    half = rows // 2

    @pl.when(odd == 1)
    def _():
        qg[0], qg[1] = qg_e[...], qg_o[...]
        st[0], st[1] = st_e[...], st_o[...]

    @pl.when(odd == 0)
    def _():
        qg[0], qg[1] = qg_o[...], qg_e[...]
        st[0], st[1] = st_o[...], st_e[...]

    biases = (
        bias_of(base, base - half, half, 2 * half, half, len_ref),
        bias_of(base + half, base + rows, half, 2 * half, half, len_ref),
    )
    for p in range(cols // PAIR):
        cs = slice(p * PAIR, (p + 1) * PAIR)
        for side in range(2):
            rs = slice(side * half, (side + 1) * half)
            qq = split_heads(qg[side, :half, cs]) * BF16(SCALE)
            gg = split_heads(qg[side, half:, cs])
            m0 = st[side, 3 * p : 3 * p + 1, :]
            l0 = st[side, 3 * p + 1 : 3 * p + 2, :]
            d0 = st[side, 3 * p + 2 : 3 * p + 3, :]
            s = nt(k_ref[rs, cs], qq) + biases[side]
            dp = nt(v_ref[rs, cs], gg)
            m = jnp.maximum(m0, jnp.max(s, axis=0, keepdims=True))
            e = jnp.exp(s - m)
            a = jnp.exp(m0 - m)
            l = a * l0 + jnp.sum(e, axis=0, keepdims=True)
            d = a * d0 + jnp.sum(e * dp, axis=0, keepdims=True)
            inv = 1.0 / jnp.maximum(l, 1.0)
            prob = e * inv
            ds = (prob * (dp - d * inv)).astype(BF16)
            dv_ref[rs, cs] = (dva_ref[rs, cs] + nn(prob.astype(BF16), gg)).astype(BF16)
            dk_ref[rs, cs] = (dka_ref[rs, cs] + nn(ds, qq)).astype(BF16)


VM = pl.BlockSpec(memory_space=pltpu.VMEM)
SM = pl.BlockSpec(memory_space=pltpu.SMEM)


def body(queries, key_vectors, value_vectors, grad_output, lengths):
    rows, cols = queries.shape
    half = rows // 2
    count = lax.axis_size("blk") * lax.axis_size("head")
    odd = lax.rem(flat_index(), 2)
    across = [(a, b) for i in range(1, count - 1, 2) for a, b in ((i, i + 1), (i + 1, i))]
    within = [(a, b) for i in range(0, count, 2) for a, b in ((i, i + 1), (i + 1, i))]

    def edges(arrays, side):
        return jnp.concatenate([lax.dynamic_slice_in_dim(x, side * half, half, 0) for x in arrays], axis=0)

    kv_o = lax.ppermute(edges((key_vectors, value_vectors), odd), AXES, across)
    kv_e = lax.ppermute(edges((key_vectors, value_vectors), 1 - odd), AXES, within)
    stats = 3 * (cols // PAIR)
    sds = jax.ShapeDtypeStruct
    params = pltpu.CompilerParams(vmem_limit_bytes=20 << 20)
    qg_o, st_o, qg_e, st_e = pl.pallas_call(
        local_kernel,
        out_shape=(sds((rows, cols), BF16), sds((stats, rows), F32)) * 2,
        in_specs=[SM] + [VM] * 4,
        out_specs=(VM,) * 4,
        compiler_params=params,
        cost_estimate=pl.CostEstimate(flops=1 << 28, bytes_accessed=2 << 20, transcendentals=1 << 18),
    )(lengths, queries, key_vectors, value_vectors, grad_output)
    qg_o, st_o = lax.ppermute(qg_o, AXES, across), lax.ppermute(st_o, AXES, across)
    qg_e, st_e = lax.ppermute(qg_e, AXES, within), lax.ppermute(st_e, AXES, within)
    dq, dk, dv = pl.pallas_call(
        own_kernel,
        out_shape=(sds((rows, cols), BF16), sds((rows, cols), F32), sds((rows, cols), F32)),
        in_specs=[SM] + [VM] * 6,
        out_specs=(VM,) * 3,
        scratch_shapes=[pltpu.VMEM((2 * rows, cols), BF16)] * 2,
        compiler_params=params,
        cost_estimate=pl.CostEstimate(flops=1 << 30, bytes_accessed=4 << 20, transcendentals=1 << 19),
    )(lengths, queries, key_vectors, value_vectors, grad_output, kv_o, kv_e)
    dk, dv = pl.pallas_call(
        edge_kernel,
        out_shape=(sds((rows, cols), BF16),) * 2,
        in_specs=[SM] + [VM] * 8,
        out_specs=(VM,) * 2,
        scratch_shapes=[pltpu.VMEM((2, rows, cols), BF16), pltpu.VMEM((2, stats, rows), F32)],
        compiler_params=params,
        cost_estimate=pl.CostEstimate(flops=1 << 27, bytes_accessed=2 << 20, transcendentals=1 << 17),
    )(lengths, key_vectors, value_vectors, qg_o, st_o, qg_e, st_e, dk, dv)
    return dq, dk, dv


def solution(mesh):
    return jax.shard_map(
        body,
        mesh=mesh,
        in_specs=(P(AXES, None),) * 4 + (P(),),
        out_specs=(P(AXES, None),) * 3,
        check_vma=False,
    )
```

```python
import jax
import jax.numpy as jnp
from jax import lax
from jax.experimental import pallas as pl
from jax.experimental.pallas import tpu as pltpu
from jax.sharding import PartitionSpec as P

DH = 64
WIN = 64
PAIR = 2 * DH
STATS = 8
SCALE = DH ** (-0.5)
NEG = -1e30
AXES = ("blk", "head")
F32 = jnp.float32
BF16 = jnp.bfloat16


def flat_index():
    return lax.axis_index("blk") * lax.axis_size("head") + lax.axis_index("head")


def recording_of(pos, len_ref):
    rec = jnp.where(pos < 0, -1, 0)
    end = jnp.int32(0)
    for r in range(len_ref.shape[0]):
        end = end + len_ref[r]
        rec = rec + jnp.where(pos >= end, 1, 0)
    return rec


def bias_of(key_first, query_first, keys, queries, lane_queries, len_ref):
    kpos = key_first + lax.broadcasted_iota(jnp.int32, (keys, 1), 0)
    qpos = query_first + lax.broadcasted_iota(jnp.int32, (1, queries), 1) % lane_queries
    near = jnp.abs(kpos - qpos) <= WIN
    same = recording_of(kpos, len_ref) == recording_of(qpos, len_ref)
    return jnp.where(near & same, 0.0, NEG).astype(F32)


def split_heads(pair):
    lane = lax.broadcasted_iota(jnp.int32, pair.shape, 1)
    zero = jnp.zeros_like(pair)
    return jnp.concatenate([jnp.where(lane < DH, pair, zero), jnp.where(lane < DH, zero, pair)], axis=0)


def nt(a, b):
    return lax.dot_general(a, b, (((1,), (1,)), ((), ())), preferred_element_type=F32)


def nn(a, b):
    return lax.dot_general(a, b, (((1,), (0,)), ((), ())), preferred_element_type=F32)


def tn(a, b):
    return lax.dot_general(a, b, (((0,), (0,)), ((), ())), preferred_element_type=F32)


def pieces(x):
    hi = x.astype(BF16).astype(F32)
    mid = (x - hi).astype(BF16).astype(F32)
    return [hi, mid, x - hi - mid]


def local_kernel(len_ref, q_ref, k_ref, v_ref, g_ref, qs_o, qs_e, own_bias, bias_o, bias_e):
    rows, cols = q_ref.shape
    me = flat_index()
    odd = lax.rem(me, 2)
    base = me * rows
    half = rows // 2
    for out, side in ((qs_o, odd), (qs_e, 1 - odd)):
        first = pl.multiple_of(side * half, half)
        out[:half, :] = q_ref[pl.ds(first, half), :] * BF16(SCALE)
        out[half:rows, :] = g_ref[pl.ds(first, half), :]
    own_bias[...] = bias_of(base - half, base, 2 * rows, rows, rows, len_ref)
    for out, side in ((bias_o, odd), (bias_e, 1 - odd)):
        out[...] = bias_of(base + side * half, base + jnp.where(side == 1, rows, -half), half, rows, half, len_ref)
    bias = own_bias[half : half + rows]
    bias = jnp.concatenate([bias, bias], axis=1)
    lane = lax.broadcasted_iota(jnp.int32, (1, rows), 1)
    for p in range(cols // PAIR):
        cs = slice(p * PAIR, (p + 1) * PAIR)
        qq = split_heads(q_ref[:, cs]) * BF16(SCALE)
        gg = split_heads(g_ref[:, cs])
        s = nt(k_ref[:, cs], qq) + bias
        dp = nt(v_ref[:, cs], gg)
        m = jnp.max(s, axis=0, keepdims=True).astype(BF16).astype(F32)
        e = jnp.exp(s - m)
        l = jnp.sum(e, axis=0, keepdims=True)
        d = jnp.sum(e * dp, axis=0, keepdims=True)
        stat = jnp.concatenate([m] + pieces(l) + pieces(d) + [jnp.zeros_like(m)], axis=0)
        a, b = stat[:, :rows], stat[:, rows:]
        lo = jnp.where(lane < half, a, pltpu.roll(b, half, 1))
        hi = jnp.where(lane < half, pltpu.roll(a, half, 1), b)
        qs_o[rows:, cs] = jnp.where(odd == 1, hi, lo).astype(BF16)
        qs_e[rows:, cs] = jnp.where(odd == 1, lo, hi).astype(BF16)


def own_kernel(bias_ref, q_ref, k_ref, v_ref, g_ref, kv_o, kv_e, dq_ref, dk_ref, dv_ref, kx, vx):
    rows, cols = q_ref.shape
    odd = lax.rem(flat_index(), 2)
    half = rows // 2
    for dst, own, o in ((kx, k_ref, 0), (vx, v_ref, half)):
        dst[half : half + rows, :] = own[...]

        @pl.when(odd == 1)
        def _():
            dst[:half, :] = kv_e[o : o + half, :]
            dst[half + rows :, :] = kv_o[o : o + half, :]

        @pl.when(odd == 0)
        def _():
            dst[:half, :] = kv_o[o : o + half, :]
            dst[half + rows :, :] = kv_e[o : o + half, :]

    bias = jnp.concatenate([bias_ref[...], bias_ref[...]], axis=1)
    lane = lax.broadcasted_iota(jnp.int32, (rows, PAIR), 1)
    for p in range(cols // PAIR):
        cs = slice(p * PAIR, (p + 1) * PAIR)
        qq = split_heads(q_ref[:, cs]) * BF16(SCALE)
        gg = split_heads(g_ref[:, cs])
        kp = kx[:, cs]
        s = nt(kp, qq) + bias
        dp = nt(vx[:, cs], gg)
        m = jnp.max(s, axis=0, keepdims=True)
        e = jnp.exp(s - m)
        inv = 1.0 / jnp.sum(e, axis=0, keepdims=True)
        prob = e * inv
        delta = jnp.sum(prob * dp, axis=0, keepdims=True)
        ds = (prob * (dp - delta)).astype(BF16)
        dv_ref[:, cs] = nn(prob[half : half + rows].astype(BF16), gg)
        dk_ref[:, cs] = nn(ds[half : half + rows], qq)
        dq2 = tn(ds, kp)
        dq_ref[:, cs] = (jnp.where(lane < DH, dq2[:rows], dq2[rows:]) * SCALE).astype(BF16)


def edge_kernel(bias_o, bias_e, k_ref, v_ref, qs_o, qs_e, dka_ref, dva_ref, dk_ref, dv_ref):
    rows, cols = k_ref.shape
    odd = lax.rem(flat_index(), 2)
    half = rows // 2
    sides = []
    for qs, bias, side in ((qs_o, bias_o, odd), (qs_e, bias_e, 1 - odd)):
        sides.append((qs, bias[...], pl.ds(pl.multiple_of(side * half, half), half)))
    items = [(slice(p * PAIR, (p + 1) * PAIR),) + side for p in range(cols // PAIR) for side in sides]
    scored = []
    for cs, qs, bias, rs in items:
        qq, gg = split_heads(qs[:half, cs]), split_heads(qs[half:rows, cs])
        scored.append((qq, gg, nt(k_ref[rs, cs], qq), nt(v_ref[rs, cs], gg)))
    graded = []
    for (cs, qs, bias, rs), (qq, gg, s, dp) in zip(items, scored):
        stat = qs[rows:, cs].astype(F32)
        m0 = stat[0:1]
        l0 = stat[1:2] + stat[2:3] + stat[3:4]
        d0 = stat[4:5] + stat[5:6] + stat[6:7]
        s = s + bias
        m = jnp.maximum(m0, jnp.max(s, axis=0, keepdims=True))
        e = jnp.exp(s - m)
        a = jnp.exp(m0 - m)
        l = a * l0 + jnp.sum(e, axis=0, keepdims=True)
        d = a * d0 + jnp.sum(e * dp, axis=0, keepdims=True)
        inv = 1.0 / jnp.where(l > 0, l, 1.0)
        prob = e * inv
        graded.append((qq, gg, prob.astype(BF16), (prob * (dp - d * inv)).astype(BF16)))
    for (cs, qs, bias, rs), (qq, gg, prob, ds) in zip(items, graded):
        dv_ref[rs, cs] = (dva_ref[rs, cs] + nn(prob, gg)).astype(BF16)
        dk_ref[rs, cs] = (dka_ref[rs, cs] + nn(ds, qq)).astype(BF16)


VM = pl.BlockSpec(memory_space=pltpu.VMEM)
SM = pl.BlockSpec(memory_space=pltpu.SMEM)


def body(queries, key_vectors, value_vectors, grad_output, lengths):
    rows, cols = queries.shape
    half = rows // 2
    count = lax.axis_size("blk") * lax.axis_size("head")
    odd = lax.rem(flat_index(), 2)
    across = [(a, b) for i in range(1, count - 1, 2) for a, b in ((i, i + 1), (i + 1, i))]
    within = [(a, b) for i in range(0, count, 2) for a, b in ((i, i + 1), (i + 1, i))]

    def edges(arrays, side):
        return jnp.concatenate([lax.dynamic_slice_in_dim(x, side * half, half, 0) for x in arrays], axis=0)

    kv_o = lax.ppermute(edges((key_vectors, value_vectors), odd), AXES, across)
    kv_e = lax.ppermute(edges((key_vectors, value_vectors), 1 - odd), AXES, within)
    sds = jax.ShapeDtypeStruct
    params = pltpu.CompilerParams(vmem_limit_bytes=20 << 20)
    sent, edge = sds((rows + STATS, cols), BF16), sds((half, rows), F32)
    qs_o, qs_e, own_bias, bias_o, bias_e = pl.pallas_call(
        local_kernel,
        out_shape=(sent, sent, sds((2 * rows, rows), F32), edge, edge),
        in_specs=[SM] + [VM] * 4,
        out_specs=(VM,) * 5,
        compiler_params=params,
        cost_estimate=pl.CostEstimate(flops=1 << 28, bytes_accessed=2 << 20, transcendentals=1 << 18),
    )(lengths, queries, key_vectors, value_vectors, grad_output)
    qs_o = lax.ppermute(qs_o, AXES, across)
    qs_e = lax.ppermute(qs_e, AXES, within)
    dq, dk, dv = pl.pallas_call(
        own_kernel,
        out_shape=(sds((rows, cols), BF16), sds((rows, cols), F32), sds((rows, cols), F32)),
        in_specs=[VM] * 7,
        out_specs=(VM,) * 3,
        scratch_shapes=[pltpu.VMEM((2 * rows, cols), BF16)] * 2,
        compiler_params=params,
        cost_estimate=pl.CostEstimate(flops=1 << 30, bytes_accessed=4 << 20, transcendentals=1 << 19),
    )(own_bias, queries, key_vectors, value_vectors, grad_output, kv_o, kv_e)
    dk, dv = pl.pallas_call(
        edge_kernel,
        out_shape=(sds((rows, cols), BF16),) * 2,
        in_specs=[VM] * 8,
        out_specs=(VM,) * 2,
        compiler_params=params,
        cost_estimate=pl.CostEstimate(flops=1 << 27, bytes_accessed=2 << 20, transcendentals=1 << 17),
    )(bias_o, bias_e, key_vectors, value_vectors, qs_o, qs_e, dk, dv)
    return dq, dk, dv


def solution(mesh):
    return jax.shard_map(
        body,
        mesh=mesh,
        in_specs=(P(AXES, None),) * 4 + (P(),),
        out_specs=(P(AXES, None),) * 3,
        check_vma=False,
    )
```

```python
import functools

import jax
import jax.numpy as jnp
from jax import lax
from jax.experimental import pallas as pl
from jax.experimental.pallas import tpu as pltpu
from jax.sharding import PartitionSpec as P

DH = 64
WIN = 64
PAIR = 2 * DH
STATS = 8
OWN_GROUP = 8
SCALE = DH ** (-0.5)
NEG = -1e30
AXES = ("blk", "head")
F32 = jnp.float32
BF16 = jnp.bfloat16


def flat_index():
    return lax.axis_index("blk") * lax.axis_size("head") + lax.axis_index("head")


def recording_of(pos, len_ref):
    rec = jnp.where(pos < 0, -1, 0)
    end = jnp.int32(0)
    for r in range(len_ref.shape[0]):
        end = end + len_ref[r]
        rec = rec + jnp.where(pos >= end, 1, 0)
    return rec


def bias_of(key_first, query_first, keys, queries, lane_queries, len_ref):
    kpos = key_first + lax.broadcasted_iota(jnp.int32, (keys, 1), 0)
    qpos = query_first + lax.broadcasted_iota(jnp.int32, (1, queries), 1) % lane_queries
    near = jnp.abs(kpos - qpos) <= WIN
    same = recording_of(kpos, len_ref) == recording_of(qpos, len_ref)
    return jnp.where(near & same, 0.0, NEG).astype(F32)


def split_heads(pair):
    lane = lax.broadcasted_iota(jnp.int32, pair.shape, 1)
    zero = jnp.zeros_like(pair)
    return jnp.concatenate([jnp.where(lane < DH, pair, zero), jnp.where(lane < DH, zero, pair)], axis=0)


def nt(a, b):
    return lax.dot_general(a, b, (((1,), (1,)), ((), ())), preferred_element_type=F32)


def nn(a, b):
    return lax.dot_general(a, b, (((1,), (0,)), ((), ())), preferred_element_type=F32)


def tn(a, b):
    return lax.dot_general(a, b, (((0,), (0,)), ((), ())), preferred_element_type=F32)


def pieces(x):
    hi = x.astype(BF16).astype(F32)
    mid = (x - hi).astype(BF16).astype(F32)
    return [hi, mid, x - hi - mid]


def prep_kernel(len_hbm, k_hbm, v_hbm, k_ref, v_ref, kv_o, k_e, v_e, own_bias, bias_o, bias_e, len_ref, sems):
    copies = [
        pltpu.make_async_copy(len_hbm, len_ref, sems.at[0]),
        pltpu.make_async_copy(k_hbm, k_ref, sems.at[1]),
        pltpu.make_async_copy(v_hbm, v_ref, sems.at[2]),
    ]
    for copy in copies:
        copy.start()
    rows = k_ref.shape[0]
    half = rows // 2
    me = flat_index()
    odd = lax.rem(me, 2)
    base = me * rows
    copies[0].wait()
    own_bias[...] = bias_of(base, base, rows, rows, rows, len_ref)
    for out, side in ((bias_o, odd), (bias_e, 1 - odd)):
        mine, other = base + side * half, base + jnp.where(side == 1, rows, -half)
        out[:rows, :] = bias_of(base, mine, rows, rows, half, len_ref)
        out[rows : rows + half, :] = bias_of(other, mine, half, rows, half, len_ref)
        out[rows + half :, :] = bias_of(mine, other, half, rows, half, len_ref)
    for n, (ref, out) in enumerate(((k_ref, k_e), (v_ref, v_e))):
        copies[n + 1].wait()
        kv_o[n * half : (n + 1) * half, :] = ref[pl.ds(pl.multiple_of(odd * half, half), half), :]
        out[...] = ref[pl.ds(pl.multiple_of((1 - odd) * half, half), half), :]


def local_kernel(bias_ref, q_ref, k_ref, v_ref, g_ref, qs_o, q_e, gs_e):
    rows, cols = q_ref.shape
    odd = lax.rem(flat_index(), 2)
    half = rows // 2
    first, other = pl.multiple_of(odd * half, half), pl.multiple_of((1 - odd) * half, half)
    qs_o[:half, :] = q_ref[pl.ds(first, half), :] * BF16(SCALE)
    qs_o[half:rows, :] = g_ref[pl.ds(first, half), :]
    q_e[...] = q_ref[pl.ds(other, half), :] * BF16(SCALE)
    gs_e[:half, :] = g_ref[pl.ds(other, half), :]
    bias = bias_ref[...]
    bias = jnp.concatenate([bias, bias], axis=1)
    lane = lax.broadcasted_iota(jnp.int32, (1, rows), 1)
    for p in range(cols // PAIR):
        cs = slice(p * PAIR, (p + 1) * PAIR)
        qq = split_heads(q_ref[:, cs]) * BF16(SCALE)
        gg = split_heads(g_ref[:, cs])
        s = nt(k_ref[:, cs], qq) + bias
        dp = nt(v_ref[:, cs], gg)
        m = jnp.max(s, axis=0, keepdims=True).astype(BF16).astype(F32)
        e = jnp.exp(s - m)
        l = jnp.sum(e, axis=0, keepdims=True)
        d = jnp.sum(e * dp, axis=0, keepdims=True)
        stat = jnp.concatenate([m] + pieces(l) + pieces(d) + [jnp.zeros_like(m)], axis=0)
        a, b = stat[:, :rows], stat[:, rows:]
        lo = jnp.where(lane < half, a, pltpu.roll(b, half, 1))
        hi = jnp.where(lane < half, pltpu.roll(a, half, 1), b)
        qs_o[rows:, cs] = jnp.where(odd == 1, hi, lo).astype(BF16)
        gs_e[half:, cs] = jnp.where(odd == 1, lo, hi).astype(BF16)


def side_rows(across, half):
    odd = lax.rem(flat_index(), 2)
    return pl.ds(pl.multiple_of((odd if across else 1 - odd) * half, half), half)


def own_half(rs, group, bias_ref, q_ref, k_ref, v_ref, g_ref, kn_ref, vn_ref, dq_ref, add):
    rows = k_ref.shape[0]
    half = rows // 2
    lane = lax.broadcasted_iota(jnp.int32, (half, PAIR), 1)
    near, far = bias_ref[:rows, :], bias_ref[rows : rows + half, :]
    scored = []
    for cs in group:
        qq = split_heads(q_ref[rs, cs]) * BF16(SCALE)
        gg = split_heads(g_ref[rs, cs])
        s = nt(k_ref[:, cs], qq), nt(kn_ref[:, cs], qq)
        dp = nt(v_ref[:, cs], gg), nt(vn_ref[:, cs], gg)
        scored.append((qq, gg, s, dp))
    graded = []
    for qq, gg, s, dp in scored:
        s = s[0] + near, s[1] + far
        m = jnp.maximum(jnp.max(s[0], axis=0, keepdims=True), jnp.max(s[1], axis=0, keepdims=True))
        e = [jnp.exp(x - m) for x in s]
        inv = 1.0 / (jnp.sum(e[0], axis=0, keepdims=True) + jnp.sum(e[1], axis=0, keepdims=True))
        prob = [x * inv for x in e]
        delta = jnp.sum(prob[0] * dp[0], axis=0, keepdims=True) + jnp.sum(prob[1] * dp[1], axis=0, keepdims=True)
        ds = [(x * (y - delta)).astype(BF16) for x, y in zip(prob, dp)]
        graded.append((qq, gg, prob[0].astype(BF16), ds))
    for cs, (qq, gg, prob, ds) in zip(group, graded):
        add(cs, nn(ds[0], qq), nn(prob, gg))
        dq2 = tn(ds[0], k_ref[:, cs]) + tn(ds[1], kn_ref[:, cs])
        dq_ref[:, cs] = (jnp.where(lane < DH, dq2[:half], dq2[half:]) * SCALE).astype(BF16)


def edge(rs, group, bias_ref, k_ref, v_ref, qn_ref, gs_ref, add):
    rows = k_ref.shape[0]
    half = rows // 2
    bias = bias_ref[rows + half :, :]
    scored = []
    for cs in group:
        qq, gg = split_heads(qn_ref[:, cs]), split_heads(gs_ref[:half, cs])
        scored.append((qq, gg, nt(k_ref[rs, cs], qq), nt(v_ref[rs, cs], gg)))
    graded = []
    for cs, (qq, gg, s, dp) in zip(group, scored):
        stat = gs_ref[half:, cs].astype(F32)
        m0 = stat[0:1]
        l0 = stat[1:2] + stat[2:3] + stat[3:4]
        d0 = stat[4:5] + stat[5:6] + stat[6:7]
        s = s + bias
        m = jnp.maximum(m0, jnp.max(s, axis=0, keepdims=True))
        e = jnp.exp(s - m)
        a = jnp.exp(m0 - m)
        l = a * l0 + jnp.sum(e, axis=0, keepdims=True)
        d = a * d0 + jnp.sum(e * dp, axis=0, keepdims=True)
        inv = 1.0 / jnp.where(l > 0, l, 1.0)
        prob = e * inv
        graded.append((qq, gg, prob.astype(BF16), (prob * (dp - d * inv)).astype(BF16)))
    for cs, (qq, gg, prob, ds) in zip(group, graded):
        add(cs, nn(ds, qq), nn(prob, gg))


def groups(cols, size):
    pairs = [slice(p * PAIR, (p + 1) * PAIR) for p in range(cols // PAIR)]
    return [pairs[i : i + size] for i in range(0, len(pairs), size)]


def flush(triples):
    copies = [pltpu.make_async_copy(*t) for t in triples]
    for copy in copies:
        copy.start()
    return copies


def within_kernel(bias_ref, q_ref, k_ref, v_ref, g_ref, kn_ref, vn_ref, qn_ref, gs_ref, dq_out, dk_ref, dv_ref, dq_ref, sems):
    rows, cols = k_ref.shape
    rs = side_rows(False, rows // 2)

    def put(cs, dk, dv):
        dk_ref[:, cs] = dk
        dv_ref[:, cs] = dv

    def add(cs, dk, dv):
        dk_ref[rs, cs] = dk_ref[rs, cs] + dk
        dv_ref[rs, cs] = dv_ref[rs, cs] + dv

    for group in groups(cols, OWN_GROUP):
        own_half(rs, group, bias_ref, q_ref, k_ref, v_ref, g_ref, kn_ref, vn_ref, dq_ref, put)
    copies = flush([(dq_ref, dq_out.at[rs], sems.at[0])])
    for group in groups(cols, 8):
        edge(rs, group, bias_ref, k_ref, v_ref, qn_ref, gs_ref, add)
    for copy in copies:
        copy.wait()


def across_kernel(bias_ref, q_ref, k_ref, v_ref, g_ref, kv_ref, dka_ref, dva_ref, dq_in, dq_out, dk_out, dv_out, dk_ref, dv_ref, dq_ref, dkn_ref, dvn_ref, sems):
    rows, cols = k_ref.shape
    half = rows // 2
    rs, rest = side_rows(True, half), side_rows(False, half)
    odd = lax.rem(flat_index(), 2)

    def put(cs, dk, dv):
        for part, acc, mine, other in ((dk, dka_ref, dk_ref, dkn_ref), (dv, dva_ref, dv_ref, dvn_ref)):
            part = part + acc[:, cs]
            low, high = part[:half], part[half:]
            mine[:, cs] = jnp.where(odd == 1, high, low)
            other[:, cs] = jnp.where(odd == 1, low, high).astype(BF16)

    for group in groups(cols, OWN_GROUP):
        own_half(rs, group, bias_ref, q_ref, k_ref, v_ref, g_ref, kv_ref.at[:half], kv_ref.at[half:], dq_ref, put)
    copies = flush([(dq_ref, dq_out.at[rs], sems.at[0]), (dkn_ref, dk_out.at[rest], sems.at[1]), (dvn_ref, dv_out.at[rest], sems.at[2])])
    for copy in copies:
        copy.wait()


def last_kernel(bias_ref, k_ref, v_ref, qs_ref, dka_ref, dva_ref, dk_in, dv_in, dk_out, dv_out, dk_ref, dv_ref, sems):
    rows, cols = k_ref.shape
    rs = side_rows(True, rows // 2)

    def put(cs, dk, dv):
        dv_ref[:, cs] = (dva_ref[:, cs] + dv).astype(BF16)
        dk_ref[:, cs] = (dka_ref[:, cs] + dk).astype(BF16)

    for group in groups(cols, 8):
        edge(rs, group, bias_ref, k_ref, v_ref, qs_ref.at[: rows // 2], qs_ref.at[rows // 2 :], put)
    copies = flush([(dk_ref, dk_out.at[rs], sems.at[0]), (dv_ref, dv_out.at[rs], sems.at[1])])
    for copy in copies:
        copy.wait()


VM = pl.BlockSpec(memory_space=pltpu.VMEM)
HB = pl.BlockSpec(memory_space=pl.ANY)


def body(queries, key_vectors, value_vectors, grad_output, lengths):
    rows, cols = queries.shape
    half = rows // 2
    count = lax.axis_size("blk") * lax.axis_size("head")
    across = [(a, b) for i in range(1, count - 1, 2) for a, b in ((i, i + 1), (i + 1, i))]
    within = [(a, b) for i in range(0, count, 2) for a, b in ((i, i + 1), (i + 1, i))]

    sds = jax.ShapeDtypeStruct
    whole, part, sent = sds((rows, cols), BF16), sds((half, cols), F32), sds((rows + STATS, cols), BF16)
    low_s, sent_e = sds((half, cols), BF16), sds((half + STATS, cols), BF16)
    masks = sds((2 * rows, rows), F32)
    low = pltpu.VMEM((half, cols), BF16)
    dma = pltpu.SemaphoreType.DMA((3,))

    def call(kernel, out_shape, in_specs, out_specs, scratch, flops, alias={}):
        return pl.pallas_call(
            kernel,
            out_shape=out_shape,
            in_specs=in_specs,
            out_specs=out_specs,
            scratch_shapes=scratch,
            input_output_aliases=alias,
            compiler_params=pltpu.CompilerParams(vmem_limit_bytes=20 << 20),
            cost_estimate=pl.CostEstimate(flops=flops, bytes_accessed=max(flops >> 10, 1), transcendentals=0),
        )

    k, v, kv_o, k_e, v_e, own_bias, bias_o, bias_e = call(
        prep_kernel,
        (whole,) * 3 + (low_s, low_s, sds((rows, rows), F32), masks, masks),
        [HB] * 3,
        (VM,) * 8,
        [pltpu.SMEM(lengths.shape, jnp.int32), dma],
        1 << 20,
    )(*(pltpu.with_memory_space_constraint(x, pltpu.HBM) for x in (lengths, key_vectors, value_vectors)))
    kv_o = lax.ppermute(kv_o, AXES, across)
    k_e = lax.ppermute(k_e, AXES, within)
    v_e = lax.ppermute(v_e, AXES, within)
    q, g = queries, grad_output
    qs_o, q_e, gs_e = call(local_kernel, (sent, low_s, sent_e), [VM] * 5, (VM,) * 3, [], 1 << 28)(own_bias, q, k, v, g)
    qs_o = lax.ppermute(qs_o, AXES, across)
    q_e = lax.ppermute(q_e, AXES, within)
    gs_e = lax.ppermute(gs_e, AXES, within)
    acc = sds((rows, cols), F32)
    dq, dk, dv = call(within_kernel, (whole, acc, acc), [VM] * 9, (HB, VM, VM), [low, dma], 0)(
        bias_e, q, k, v, g, k_e, v_e, q_e, gs_e
    )
    dq, dk_out, dv_out, dk, dv = call(
        across_kernel, (whole,) * 3 + (part,) * 2, [VM] * 8 + [HB], (HB,) * 3 + (VM,) * 2, [low] * 3 + [dma], 1 << 31, {8: 0}
    )(bias_o, q, k, v, g, kv_o, dk, dv, dq)
    dk, dv = call(last_kernel, (whole,) * 2, [VM] * 6 + [HB] * 2, (HB,) * 2, [low] * 2 + [dma], 1 << 27, {6: 0, 7: 1})(
        bias_o, k, v, qs_o, dk, dv, dk_out, dv_out
    )
    return dq, dk, dv


def solution(mesh):
    return jax.shard_map(
        body,
        mesh=mesh,
        in_specs=(P(AXES, None),) * 4 + (P(),),
        out_specs=(P(AXES, None),) * 3,
        check_vma=False,
    )
```

```python
import functools

import jax
import jax.numpy as jnp
from jax import lax
from jax.experimental import pallas as pl
from jax.experimental.pallas import tpu as pltpu
from jax.sharding import PartitionSpec as P

DH = 64
WIN = 64
PAIR = 2 * DH
STATS = 8
MOVED = 16
COSTS = (1 << 28, 0, 1 << 31, 0, 1 << 27)
LAST = 2
SCALE = DH ** (-0.5)
NEG = -1e30
AXES = ("blk", "head")
F32 = jnp.float32
BF16 = jnp.bfloat16


def flat_index():
    return lax.axis_index("blk") * lax.axis_size("head") + lax.axis_index("head")


def recording_of(pos, len_ref):
    rec = jnp.where(pos < 0, -1, 0)
    end = jnp.int32(0)
    for r in range(len_ref.shape[0]):
        end = end + len_ref[r]
        rec = rec + jnp.where(pos >= end, 1, 0)
    return rec


def bias_of(key_first, query_first, keys, queries, lane_queries, len_ref):
    kpos = key_first + lax.broadcasted_iota(jnp.int32, (keys, 1), 0)
    qpos = query_first + lax.broadcasted_iota(jnp.int32, (1, queries), 1) % lane_queries
    near = jnp.abs(kpos - qpos) <= WIN
    same = recording_of(kpos, len_ref) == recording_of(qpos, len_ref)
    return jnp.where(near & same, 0.0, NEG).astype(F32)


def split_heads(pair):
    lane = lax.broadcasted_iota(jnp.int32, pair.shape, 1)
    zero = jnp.zeros_like(pair)
    return jnp.concatenate([jnp.where(lane < DH, pair, zero), jnp.where(lane < DH, zero, pair)], axis=0)


def nt(a, b):
    return lax.dot_general(a, b, (((1,), (1,)), ((), ())), preferred_element_type=F32)


def nn(a, b):
    return lax.dot_general(a, b, (((1,), (0,)), ((), ())), preferred_element_type=F32)


def tn(a, b):
    return lax.dot_general(a, b, (((0,), (0,)), ((), ())), preferred_element_type=F32)


def pieces(x):
    hi = x.astype(BF16).astype(F32)
    mid = (x - hi).astype(BF16).astype(F32)
    return [hi, mid, x - hi - mid]


def prep_kernel(len_hbm, k_hbm, v_hbm, k_ref, v_ref, kv_o, kv_e, own_bias, bias_o, bias_e, len_ref, sems):
    copies = [
        pltpu.make_async_copy(len_hbm, len_ref, sems.at[0]),
        pltpu.make_async_copy(k_hbm, k_ref, sems.at[1]),
        pltpu.make_async_copy(v_hbm, v_ref, sems.at[2]),
    ]
    for copy in copies:
        copy.start()
    rows = k_ref.shape[0]
    half = rows // 2
    me = flat_index()
    odd = lax.rem(me, 2)
    base = me * rows
    copies[0].wait()
    own_bias[...] = bias_of(base, base, rows, rows, rows, len_ref)
    for out, side in ((bias_o, odd), (bias_e, 1 - odd)):
        mine, other = base + side * half, base + jnp.where(side == 1, rows, -half)
        out[:rows, :] = bias_of(base, mine, rows, rows, half, len_ref)
        out[rows : rows + half, :] = bias_of(other, mine, half, rows, half, len_ref)
        out[rows + half :, :] = bias_of(mine, other, half, rows, half, len_ref)
    for n, ref in enumerate((k_ref, v_ref)):
        copies[n + 1].wait()
        kv_o[n * half : (n + 1) * half, :] = ref[pl.ds(pl.multiple_of(odd * half, half), half), :]
        size = half - n * MOVED
        kv_e[n * half : n * half + size, :] = ref[pl.ds(pl.multiple_of((1 - odd) * half, half), size), :]


def local_kernel(bias_ref, q_ref, k_ref, v_ref, g_ref, qs_1, qs_2, q_e, gs_e):
    rows, cols = q_ref.shape
    odd = lax.rem(flat_index(), 2)
    half = rows // 2
    first, other = pl.multiple_of(odd * half, half), pl.multiple_of((1 - odd) * half, half)
    cut = qs_1.shape[1]
    for out, cs in ((qs_1, slice(0, cut)), (qs_2, slice(cut, cols))):
        out[:half, :] = q_ref[pl.ds(first, half), cs] * BF16(SCALE)
        out[half:rows, :] = g_ref[pl.ds(first, half), cs]
    q_e[:half, :] = q_ref[pl.ds(other, half), :] * BF16(SCALE)
    q_e[half:, :] = v_ref[pl.ds(pl.multiple_of(other + half - MOVED, MOVED), MOVED), :]
    gs_e[:half, :] = g_ref[pl.ds(other, half), :]
    bias = bias_ref[...]
    bias = jnp.concatenate([bias, bias], axis=1)
    lane = lax.broadcasted_iota(jnp.int32, (1, rows), 1)
    for p in range(cols // PAIR):
        cs = slice(p * PAIR, (p + 1) * PAIR)
        qq = split_heads(q_ref[:, cs]) * BF16(SCALE)
        gg = split_heads(g_ref[:, cs])
        s = nt(k_ref[:, cs], qq) + bias
        dp = nt(v_ref[:, cs], gg)
        m = jnp.max(s, axis=0, keepdims=True).astype(BF16).astype(F32)
        e = jnp.exp(s - m)
        l = jnp.sum(e, axis=0, keepdims=True)
        d = jnp.sum(e * dp, axis=0, keepdims=True)
        stat = jnp.concatenate([m] + pieces(l) + pieces(d) + [jnp.zeros_like(m)], axis=0)
        a, b = stat[:, :rows], stat[:, rows:]
        lo = jnp.where(lane < half, a, pltpu.roll(b, half, 1))
        hi = jnp.where(lane < half, pltpu.roll(a, half, 1), b)
        out, start = (qs_1, p * PAIR) if p * PAIR < cut else (qs_2, p * PAIR - cut)
        out[rows:, start : start + PAIR] = jnp.where(odd == 1, hi, lo).astype(BF16)
        gs_e[half:, cs] = jnp.where(odd == 1, lo, hi).astype(BF16)


def side_rows(across, half):
    odd = lax.rem(flat_index(), 2)
    return pl.ds(pl.multiple_of((odd if across else 1 - odd) * half, half), half)


def own_half(rs, group, bias_ref, q_ref, k_ref, v_ref, g_ref, kn_ref, v_near, dq_ref, add):
    rows = k_ref.shape[0]
    half = rows // 2
    lane = lax.broadcasted_iota(jnp.int32, (half, PAIR), 1)
    near, far = bias_ref[:rows, :], bias_ref[rows : rows + half, :]
    scored = []
    for cs in group:
        qq = split_heads(q_ref[rs, cs]) * BF16(SCALE)
        gg = split_heads(g_ref[rs, cs])
        s = nt(k_ref[:, cs], qq), nt(kn_ref[:, cs], qq)
        dp = nt(v_ref[:, cs], gg), nt(v_near(cs), gg)
        scored.append((qq, gg, s, dp))
    graded = []
    for qq, gg, s, dp in scored:
        s = s[0] + near, s[1] + far
        m = jnp.maximum(jnp.max(s[0], axis=0, keepdims=True), jnp.max(s[1], axis=0, keepdims=True))
        e = [jnp.exp(x - m) for x in s]
        inv = 1.0 / (jnp.sum(e[0], axis=0, keepdims=True) + jnp.sum(e[1], axis=0, keepdims=True))
        prob = [x * inv for x in e]
        delta = jnp.sum(prob[0] * dp[0], axis=0, keepdims=True) + jnp.sum(prob[1] * dp[1], axis=0, keepdims=True)
        ds = [(x * (y - delta)).astype(BF16) for x, y in zip(prob, dp)]
        graded.append((qq, gg, prob[0].astype(BF16), ds))
    for cs, (qq, gg, prob, ds) in zip(group, graded):
        add(cs, nn(ds[0], qq), nn(prob, gg))
        dq2 = tn(ds[0], k_ref[:, cs]) + tn(ds[1], kn_ref[:, cs])
        dq_ref[:, cs] = (jnp.where(lane < DH, dq2[:half], dq2[half:]) * SCALE).astype(BF16)


def edge(rs, group, first, bias_ref, k_ref, v_ref, qn_ref, gs_ref, add):
    rows = k_ref.shape[0]
    half = rows // 2
    bias = bias_ref[rows + half :, :]
    scored = []
    for cs in group:
        ns = slice(cs.start - first, cs.stop - first)
        qq, gg = split_heads(qn_ref[:, ns]), split_heads(gs_ref[:half, ns])
        scored.append((qq, gg, nt(k_ref[rs, cs], qq), nt(v_ref[rs, cs], gg)))
    graded = []
    for cs, (qq, gg, s, dp) in zip(group, scored):
        stat = gs_ref[half:, cs.start - first : cs.stop - first].astype(F32)
        m0 = stat[0:1]
        l0 = stat[1:2] + stat[2:3] + stat[3:4]
        d0 = stat[4:5] + stat[5:6] + stat[6:7]
        s = s + bias
        m = jnp.maximum(m0, jnp.max(s, axis=0, keepdims=True))
        e = jnp.exp(s - m)
        a = jnp.exp(m0 - m)
        l = a * l0 + jnp.sum(e, axis=0, keepdims=True)
        d = a * d0 + jnp.sum(e * dp, axis=0, keepdims=True)
        inv = 1.0 / jnp.where(l > 0, l, 1.0)
        prob = e * inv
        graded.append((qq, gg, prob.astype(BF16), (prob * (dp - d * inv)).astype(BF16)))
    for cs, (qq, gg, prob, ds) in zip(group, graded):
        add(cs, nn(ds, qq), nn(prob, gg))


def pairs_of(first, end):
    return [slice(c, c + PAIR) for c in range(first, end, PAIR)]


def within_kernel(bias_ref, q_ref, k_ref, v_ref, g_ref, kv_ref, qn_ref, gs_ref, dq_ref, dk_ref, dv_ref):
    rows, cols = k_ref.shape
    half = rows // 2
    rs = side_rows(False, half)

    def put(cs, dk, dv):
        dk_ref[:, cs] = dk
        dv_ref[:, cs] = dv

    def add(cs, dk, dv):
        dk_ref[rs, cs] = dk_ref[rs, cs] + dk
        dv_ref[rs, cs] = dv_ref[rs, cs] + dv

    kn_ref = kv_ref.at[:half]

    def vn_ref(cs):
        return jnp.concatenate([kv_ref[half:, cs], qn_ref[half:, cs]], axis=0)

    own_half(rs, pairs_of(0, cols), bias_ref, q_ref, k_ref, v_ref, g_ref, kn_ref, vn_ref, dq_ref, put)
    edge(rs, pairs_of(0, cols), 0, bias_ref, k_ref, v_ref, qn_ref.at[:half], gs_ref, add)


def across_kernel(bias_ref, q_ref, k_ref, v_ref, g_ref, kv_ref, dka_ref, dva_ref, dq_ref, dkn_ref, dvn_ref, dk_ref, dv_ref):
    rows, cols = k_ref.shape
    half = rows // 2
    odd = lax.rem(flat_index(), 2)

    def put(cs, dk, dv):
        for part, acc, mine, other in ((dk, dka_ref, dk_ref, dkn_ref), (dv, dva_ref, dv_ref, dvn_ref)):
            part = part + acc[:, cs]
            low, high = part[:half], part[half:]
            mine[:, cs] = jnp.where(odd == 1, high, low)
            other[:, cs] = jnp.where(odd == 1, low, high).astype(BF16)

    own_half(
        side_rows(True, half),
        pairs_of(0, cols),
        bias_ref,
        q_ref,
        k_ref,
        v_ref,
        g_ref,
        kv_ref.at[:half],
        lambda cs: kv_ref[half:, cs],
        dq_ref,
        put,
    )


def edge_into(first, bias_ref, k_ref, v_ref, qs_ref, dka_ref, dva_ref, dk_ref, dv_ref):
    half = k_ref.shape[0] // 2
    size = qs_ref.shape[1]

    def put(cs, dk, dv):
        to = slice(cs.start - first, cs.stop - first)
        dv_ref[:, to] = (dva_ref[:, cs] + dv).astype(BF16)
        dk_ref[:, to] = (dka_ref[:, cs] + dk).astype(BF16)

    edge(
        side_rows(True, half),
        pairs_of(first, first + size),
        first,
        bias_ref,
        k_ref,
        v_ref,
        qs_ref.at[:half],
        qs_ref.at[half:],
        put,
    )


def first_edge_kernel(bias_ref, k_ref, v_ref, qs_ref, dka_ref, dva_ref, dk_ref, dv_ref):
    edge_into(0, bias_ref, k_ref, v_ref, qs_ref, dka_ref, dva_ref, dk_ref, dv_ref)


def last_kernel(
    bias_ref, k_ref, v_ref, qs_ref, dka_ref, dva_ref, dqn, dqm, dkn, dvn, dk1, dv1, dq_out, dk_out, dv_out, dk2, dv2, sems
):
    rows, cols = k_ref.shape
    half = rows // 2
    mine, other = side_rows(True, half), side_rows(False, half)
    first = cols - qs_ref.shape[1]
    early = [
        (dqn, dq_out.at[other]),
        (dqm, dq_out.at[mine]),
        (dkn, dk_out.at[other]),
        (dvn, dv_out.at[other]),
        (dk1, dk_out.at[mine, :first]),
        (dv1, dv_out.at[mine, :first]),
    ]
    late = [(dk2, dk_out.at[mine, first:]), (dv2, dv_out.at[mine, first:])]
    copies = [pltpu.make_async_copy(a, b, sems.at[n]) for n, (a, b) in enumerate(early + late)]
    for copy in copies[: len(early)]:
        copy.start()
    edge_into(first, bias_ref, k_ref, v_ref, qs_ref, dka_ref, dva_ref, dk2, dv2)
    for copy in copies[len(early) :]:
        copy.start()
    for copy in copies:
        copy.wait()


VM = pl.BlockSpec(memory_space=pltpu.VMEM)
HB = pl.BlockSpec(memory_space=pl.ANY)


def body(queries, key_vectors, value_vectors, grad_output, lengths):
    rows, cols = queries.shape
    half = rows // 2
    count = lax.axis_size("blk") * lax.axis_size("head")
    across = [(a, b) for i in range(1, count - 1, 2) for a, b in ((i, i + 1), (i + 1, i))]
    within = [(a, b) for i in range(0, count, 2) for a, b in ((i, i + 1), (i + 1, i))]

    sds = jax.ShapeDtypeStruct
    whole, part = sds((rows, cols), BF16), sds((half, cols), F32)
    low_s = sds((half, cols), BF16)
    sent_q, sent_g = sds((half + MOVED, cols), BF16), sds((half + STATS, cols), BF16)
    masks = sds((2 * rows, rows), F32)
    dma = pltpu.SemaphoreType.DMA((3,))

    def call(kernel, out_shape, in_specs, out_specs, scratch, flops):
        return pl.pallas_call(
            kernel,
            out_shape=out_shape,
            in_specs=in_specs,
            out_specs=out_specs,
            scratch_shapes=scratch,
            compiler_params=pltpu.CompilerParams(vmem_limit_bytes=20 << 20),
            cost_estimate=pl.CostEstimate(flops=flops, bytes_accessed=max(flops >> 10, 1), transcendentals=0),
        )

    k, v, kv_o, kv_e, own_bias, bias_o, bias_e = call(
        prep_kernel,
        (whole,) * 3 + (sds((rows - MOVED, cols), BF16), sds((rows, rows), F32), masks, masks),
        [HB] * 3,
        (VM,) * 7,
        [pltpu.SMEM(lengths.shape, jnp.int32), dma],
        1 << 20,
    )(*(pltpu.with_memory_space_constraint(x, pltpu.HBM) for x in (lengths, key_vectors, value_vectors)))
    kv_o = lax.ppermute(kv_o, AXES, across)
    kv_e = lax.ppermute(kv_e, AXES, within)
    q, g = queries, grad_output
    cut = cols - LAST * PAIR
    qs_1, qs_2, q_e, gs_e = call(
        local_kernel,
        (sds((rows + STATS, cut), BF16), sds((rows + STATS, cols - cut), BF16), sent_q, sent_g),
        [VM] * 5,
        (VM,) * 4,
        [],
        COSTS[0],
    )(own_bias, q, k, v, g)
    qs_1 = lax.ppermute(qs_1, AXES, across)
    qs_2 = lax.ppermute(qs_2, AXES, across)
    q_e = lax.ppermute(q_e, AXES, within)
    gs_e = lax.ppermute(gs_e, AXES, within)
    acc = sds((rows, cols), F32)
    dqn, dk, dv = call(within_kernel, (low_s, acc, acc), [VM] * 8, (VM,) * 3, [], COSTS[1])(
        bias_e, q, k, v, g, kv_e, q_e, gs_e
    )
    dqm, dkn, dvn, dk, dv = call(across_kernel, (low_s,) * 3 + (part,) * 2, [VM] * 8, (VM,) * 5, [], COSTS[2])(
        bias_o, q, k, v, g, kv_o, dk, dv
    )
    done = sds((half, cut), BF16)
    dk1, dv1 = call(first_edge_kernel, (done, done), [VM] * 6, (VM,) * 2, [], COSTS[3])(bias_o, k, v, qs_1, dk, dv)
    rest = pltpu.VMEM((half, cols - cut), BF16)
    return call(
        last_kernel, (whole,) * 3, [VM] * 12, (HB,) * 3, [rest, rest, pltpu.SemaphoreType.DMA((8,))], COSTS[4]
    )(bias_o, k, v, qs_2, dk, dv, dqn, dqm, dkn, dvn, dk1, dv1)


def solution(mesh):
    return jax.shard_map(
        body,
        mesh=mesh,
        in_specs=(P(AXES, None),) * 4 + (P(),),
        out_specs=(P(AXES, None),) * 3,
        check_vma=False,
    )
```

```python
import functools

import jax
import jax.numpy as jnp
from jax import lax
from jax.experimental import pallas as pl
from jax.experimental.pallas import tpu as pltpu
from jax.sharding import PartitionSpec as P

DH = 64
WIN = 64
PAIR = 2 * DH
STATS = 8
FAR_STATS = (0, 1, 2, 4, 5, 6)
MOVED = 16
COSTS = (1 << 28, 0, 1 << 31, 0, 1 << 27)
LAST = 2
SCALE = DH ** (-0.5)
NEG = -1e30
AXES = ("blk", "head")
F32 = jnp.float32
BF16 = jnp.bfloat16


def flat_index():
    return lax.axis_index("blk") * lax.axis_size("head") + lax.axis_index("head")


def recording_of(pos, len_ref):
    rec = jnp.where(pos < 0, -1, 0)
    end = jnp.int32(0)
    for r in range(len_ref.shape[0]):
        end = end + len_ref[r]
        rec = rec + jnp.where(pos >= end, 1, 0)
    return rec


def bias_of(key_first, query_first, keys, queries, lane_queries, len_ref):
    kpos = key_first + lax.broadcasted_iota(jnp.int32, (keys, 1), 0)
    qpos = query_first + lax.broadcasted_iota(jnp.int32, (1, queries), 1) % lane_queries
    near = jnp.abs(kpos - qpos) <= WIN
    same = recording_of(kpos, len_ref) == recording_of(qpos, len_ref)
    return jnp.where(near & same, 0.0, NEG).astype(F32)


def split_heads(pair):
    lane = lax.broadcasted_iota(jnp.int32, pair.shape, 1)
    zero = jnp.zeros_like(pair)
    return jnp.concatenate([jnp.where(lane < DH, pair, zero), jnp.where(lane < DH, zero, pair)], axis=0)


def nt(a, b):
    return lax.dot_general(a, b, (((1,), (1,)), ((), ())), preferred_element_type=F32)


def nn(a, b):
    return lax.dot_general(a, b, (((1,), (0,)), ((), ())), preferred_element_type=F32)


def tn(a, b):
    return lax.dot_general(a, b, (((0,), (0,)), ((), ())), preferred_element_type=F32)


def pieces(x):
    hi = x.astype(BF16).astype(F32)
    mid = (x - hi).astype(BF16).astype(F32)
    return [hi, mid, x - hi - mid]


def prep_kernel(len_hbm, k_hbm, v_hbm, k_ref, v_ref, kv_o, kv_e, own_bias, bias_o, bias_e, len_ref, sems):
    copies = [
        pltpu.make_async_copy(len_hbm, len_ref, sems.at[0]),
        pltpu.make_async_copy(k_hbm, k_ref, sems.at[1]),
        pltpu.make_async_copy(v_hbm, v_ref, sems.at[2]),
    ]
    for copy in copies:
        copy.start()
    rows = k_ref.shape[0]
    half = rows // 2
    me = flat_index()
    odd = lax.rem(me, 2)
    base = me * rows
    copies[0].wait()
    own_bias[...] = bias_of(base, base, rows, rows, rows, len_ref)
    for out, side in ((bias_o, odd), (bias_e, 1 - odd)):
        mine, other = base + side * half, base + jnp.where(side == 1, rows, -half)
        out[:rows, :] = bias_of(base, mine, rows, rows, half, len_ref)
        out[rows : rows + half, :] = bias_of(other, mine, half, rows, half, len_ref)
        out[rows + half :, :] = bias_of(mine, other, half, rows, half, len_ref)
    for n, ref in enumerate((k_ref, v_ref)):
        copies[n + 1].wait()
        kv_o[n * half : (n + 1) * half, :] = ref[pl.ds(pl.multiple_of(odd * half, half), half), :]
        size = half - n * MOVED
        kv_e[n * half : n * half + size, :] = ref[pl.ds(pl.multiple_of((1 - odd) * half, half), size), :]


def local_kernel(bias_ref, q_ref, k_ref, v_ref, g_ref, qs_1, qs_2, q_e, gs_e):
    rows, cols = q_ref.shape
    odd = lax.rem(flat_index(), 2)
    half = rows // 2
    first, other = pl.multiple_of(odd * half, half), pl.multiple_of((1 - odd) * half, half)
    cut = qs_1.shape[1]
    for out, cs in ((qs_1, slice(0, cut)), (qs_2, slice(cut, cols))):
        out[:half, :] = q_ref[pl.ds(first, half), cs] * BF16(SCALE)
        out[half:rows, :] = g_ref[pl.ds(first, half), cs]
    q_e[:half, :] = q_ref[pl.ds(other, half), :] * BF16(SCALE)
    q_e[half:, :] = v_ref[pl.ds(pl.multiple_of(other + half - MOVED, MOVED), MOVED), :]
    gs_e[:half, :] = g_ref[pl.ds(other, half), :]
    bias = bias_ref[...]
    bias = jnp.concatenate([bias, bias], axis=1)
    lane = lax.broadcasted_iota(jnp.int32, (1, rows), 1)
    far = []
    for p in range(cols // PAIR):
        cs = slice(p * PAIR, (p + 1) * PAIR)
        qq = split_heads(q_ref[:, cs]) * BF16(SCALE)
        gg = split_heads(g_ref[:, cs])
        s = nt(k_ref[:, cs], qq) + bias
        dp = nt(v_ref[:, cs], gg)
        m = jnp.max(s, axis=0, keepdims=True).astype(BF16).astype(F32)
        e = jnp.exp(s - m)
        l = jnp.sum(e, axis=0, keepdims=True)
        d = jnp.sum(e * dp, axis=0, keepdims=True)
        stat = jnp.concatenate([m] + pieces(l) + pieces(d) + [jnp.zeros_like(m)], axis=0)
        a, b = stat[:, :rows], stat[:, rows:]
        lo = jnp.where(lane < half, a, pltpu.roll(b, half, 1))
        hi = jnp.where(lane < half, pltpu.roll(a, half, 1), b)
        far.append(jnp.where(odd == 1, hi, lo))
        gs_e[half:, cs] = jnp.where(odd == 1, lo, hi).astype(BF16)
    for n, r in enumerate(FAR_STATS):
        block = jnp.concatenate([stat[r : r + 1] for stat in far], axis=0)
        qs_1[rows:, n * PAIR : (n + 1) * PAIR] = block.astype(BF16)


def side_rows(across, half):
    odd = lax.rem(flat_index(), 2)
    return pl.ds(pl.multiple_of((odd if across else 1 - odd) * half, half), half)


def own_half(rs, group, bias_ref, q_ref, k_ref, v_ref, g_ref, kn_ref, v_near, dq_ref, add):
    rows = k_ref.shape[0]
    half = rows // 2
    lane = lax.broadcasted_iota(jnp.int32, (half, PAIR), 1)
    near, far = bias_ref[:rows, :], bias_ref[rows : rows + half, :]
    scored = []
    for cs in group:
        qq = split_heads(q_ref[rs, cs]) * BF16(SCALE)
        gg = split_heads(g_ref[rs, cs])
        s = nt(k_ref[:, cs], qq), nt(kn_ref[:, cs], qq)
        dp = nt(v_ref[:, cs], gg), nt(v_near(cs), gg)
        scored.append((qq, gg, s, dp))
    graded = []
    for qq, gg, s, dp in scored:
        s = s[0] + near, s[1] + far
        m = jnp.maximum(jnp.max(s[0], axis=0, keepdims=True), jnp.max(s[1], axis=0, keepdims=True))
        e = [jnp.exp(x - m) for x in s]
        inv = 1.0 / (jnp.sum(e[0], axis=0, keepdims=True) + jnp.sum(e[1], axis=0, keepdims=True))
        prob = [x * inv for x in e]
        delta = jnp.sum(prob[0] * dp[0], axis=0, keepdims=True) + jnp.sum(prob[1] * dp[1], axis=0, keepdims=True)
        ds = [(x * (y - delta)).astype(BF16) for x, y in zip(prob, dp)]
        graded.append((qq, gg, prob[0].astype(BF16), ds))
    for cs, (qq, gg, prob, ds) in zip(group, graded):
        add(cs, nn(ds[0], qq), nn(prob, gg))
        dq2 = tn(ds[0], k_ref[:, cs]) + tn(ds[1], kn_ref[:, cs])
        dq_ref[:, cs] = (jnp.where(lane < DH, dq2[:half], dq2[half:]) * SCALE).astype(BF16)


def edge(rs, group, first, bias_ref, k_ref, v_ref, qn_ref, g_ref, stats, add):
    rows = k_ref.shape[0]
    half = rows // 2
    bias = bias_ref[rows + half :, :]
    scored = []
    for cs in group:
        ns = slice(cs.start - first, cs.stop - first)
        qq, gg = split_heads(qn_ref[:, ns]), split_heads(g_ref[:, ns])
        scored.append((qq, gg, nt(k_ref[rs, cs], qq), nt(v_ref[rs, cs], gg)))
    graded = []
    for cs, (qq, gg, s, dp) in zip(group, scored):
        m0, l0, d0 = stats(cs)
        s = s + bias
        m = jnp.maximum(m0, jnp.max(s, axis=0, keepdims=True))
        e = jnp.exp(s - m)
        a = jnp.exp(m0 - m)
        l = a * l0 + jnp.sum(e, axis=0, keepdims=True)
        d = a * d0 + jnp.sum(e * dp, axis=0, keepdims=True)
        inv = 1.0 / jnp.where(l > 0, l, 1.0)
        prob = e * inv
        graded.append((qq, gg, prob.astype(BF16), (prob * (dp - d * inv)).astype(BF16)))
    for cs, (qq, gg, prob, ds) in zip(group, graded):
        add(cs, nn(ds, qq), nn(prob, gg))


def pairs_of(first, end):
    return [slice(c, c + PAIR) for c in range(first, end, PAIR)]


def within_kernel(bias_ref, q_ref, k_ref, v_ref, g_ref, kv_ref, qn_ref, gs_ref, dq_ref, dk_ref, dv_ref):
    rows, cols = k_ref.shape
    half = rows // 2
    rs = side_rows(False, half)

    def put(cs, dk, dv):
        dk_ref[:, cs] = dk
        dv_ref[:, cs] = dv

    def add(cs, dk, dv):
        dk_ref[rs, cs] = dk_ref[rs, cs] + dk
        dv_ref[rs, cs] = dv_ref[rs, cs] + dv

    kn_ref = kv_ref.at[:half]

    def vn_ref(cs):
        return jnp.concatenate([kv_ref[half:, cs], qn_ref[half:, cs]], axis=0)

    own_half(rs, pairs_of(0, cols), bias_ref, q_ref, k_ref, v_ref, g_ref, kn_ref, vn_ref, dq_ref, put)

    def stats(cs):
        stat = gs_ref[half:, cs].astype(F32)
        return stat[0:1], stat[1:2] + stat[2:3] + stat[3:4], stat[4:5] + stat[5:6] + stat[6:7]

    edge(rs, pairs_of(0, cols), 0, bias_ref, k_ref, v_ref, qn_ref.at[:half], gs_ref.at[:half], stats, add)


def across_kernel(bias_ref, q_ref, k_ref, v_ref, g_ref, kv_ref, dka_ref, dva_ref, dq_ref, dkn_ref, dvn_ref, dk_ref, dv_ref):
    rows, cols = k_ref.shape
    half = rows // 2
    odd = lax.rem(flat_index(), 2)

    def put(cs, dk, dv):
        for part, acc, mine, other in ((dk, dka_ref, dk_ref, dkn_ref), (dv, dva_ref, dv_ref, dvn_ref)):
            part = part + acc[:, cs]
            low, high = part[:half], part[half:]
            mine[:, cs] = jnp.where(odd == 1, high, low)
            other[:, cs] = jnp.where(odd == 1, low, high).astype(BF16)

    own_half(
        side_rows(True, half),
        pairs_of(0, cols),
        bias_ref,
        q_ref,
        k_ref,
        v_ref,
        g_ref,
        kv_ref.at[:half],
        lambda cs: kv_ref[half:, cs],
        dq_ref,
        put,
    )


def edge_into(first, bias_ref, k_ref, v_ref, qs_ref, st_ref, dka_ref, dva_ref, dk_ref, dv_ref):
    rows = k_ref.shape[0]
    half = rows // 2
    stat = st_ref[rows:, :].astype(F32)

    def stats(cs):
        p = cs.start // PAIR
        m, l1, l2, d1, d2, d3 = (stat[p : p + 1, n * PAIR : (n + 1) * PAIR] for n in range(len(FAR_STATS)))
        return m, l1 + l2, d1 + d2 + d3

    size = qs_ref.shape[1]

    def put(cs, dk, dv):
        to = slice(cs.start - first, cs.stop - first)
        dv_ref[:, to] = (dva_ref[:, cs] + dv).astype(BF16)
        dk_ref[:, to] = (dka_ref[:, cs] + dk).astype(BF16)

    edge(
        side_rows(True, half),
        pairs_of(first, first + size),
        first,
        bias_ref,
        k_ref,
        v_ref,
        qs_ref.at[:half],
        qs_ref.at[half:rows],
        stats,
        put,
    )


def first_edge_kernel(bias_ref, k_ref, v_ref, qs_ref, dka_ref, dva_ref, dk_ref, dv_ref):
    edge_into(0, bias_ref, k_ref, v_ref, qs_ref, qs_ref, dka_ref, dva_ref, dk_ref, dv_ref)


def last_kernel(
    bias_ref, k_ref, v_ref, qs_ref, st_ref, dka_ref, dva_ref, dqn, dqm, dkn, dvn, dk1, dv1, dq_out, dk_out, dv_out, dk2, dv2, sems
):
    rows, cols = k_ref.shape
    half = rows // 2
    mine, other = side_rows(True, half), side_rows(False, half)
    first = cols - qs_ref.shape[1]
    early = [
        (dqn, dq_out.at[other]),
        (dqm, dq_out.at[mine]),
        (dkn, dk_out.at[other]),
        (dvn, dv_out.at[other]),
        (dk1, dk_out.at[mine, :first]),
        (dv1, dv_out.at[mine, :first]),
    ]
    late = [(dk2, dk_out.at[mine, first:]), (dv2, dv_out.at[mine, first:])]
    copies = [pltpu.make_async_copy(a, b, sems.at[n]) for n, (a, b) in enumerate(early + late)]
    for copy in copies[: len(early)]:
        copy.start()
    edge_into(first, bias_ref, k_ref, v_ref, qs_ref, st_ref, dka_ref, dva_ref, dk2, dv2)
    for copy in copies[len(early) :]:
        copy.start()
    for copy in copies:
        copy.wait()


VM = pl.BlockSpec(memory_space=pltpu.VMEM)
HB = pl.BlockSpec(memory_space=pl.ANY)


def body(queries, key_vectors, value_vectors, grad_output, lengths):
    rows, cols = queries.shape
    half = rows // 2
    count = lax.axis_size("blk") * lax.axis_size("head")
    across = [(a, b) for i in range(1, count - 1, 2) for a, b in ((i, i + 1), (i + 1, i))]
    within = [(a, b) for i in range(0, count, 2) for a, b in ((i, i + 1), (i + 1, i))]

    sds = jax.ShapeDtypeStruct
    whole, part = sds((rows, cols), BF16), sds((half, cols), F32)
    low_s = sds((half, cols), BF16)
    sent_q, sent_g = sds((half + MOVED, cols), BF16), sds((half + STATS, cols), BF16)
    masks = sds((2 * rows, rows), F32)
    dma = pltpu.SemaphoreType.DMA((3,))

    def call(kernel, out_shape, in_specs, out_specs, scratch, flops):
        return pl.pallas_call(
            kernel,
            out_shape=out_shape,
            in_specs=in_specs,
            out_specs=out_specs,
            scratch_shapes=scratch,
            compiler_params=pltpu.CompilerParams(vmem_limit_bytes=20 << 20),
            cost_estimate=pl.CostEstimate(flops=flops, bytes_accessed=max(flops >> 10, 1), transcendentals=0),
        )

    k, v, kv_o, kv_e, own_bias, bias_o, bias_e = call(
        prep_kernel,
        (whole,) * 3 + (sds((rows - MOVED, cols), BF16), sds((rows, rows), F32), masks, masks),
        [HB] * 3,
        (VM,) * 7,
        [pltpu.SMEM(lengths.shape, jnp.int32), dma],
        1 << 20,
    )(*(pltpu.with_memory_space_constraint(x, pltpu.HBM) for x in (lengths, key_vectors, value_vectors)))
    kv_o = lax.ppermute(kv_o, AXES, across)
    kv_e = lax.ppermute(kv_e, AXES, within)
    q, g = queries, grad_output
    cut = cols - LAST * PAIR
    qs_1, qs_2, q_e, gs_e = call(
        local_kernel,
        (sds((rows + STATS, cut), BF16), sds((rows, cols - cut), BF16), sent_q, sent_g),
        [VM] * 5,
        (VM,) * 4,
        [],
        COSTS[0],
    )(own_bias, q, k, v, g)
    qs_1 = lax.ppermute(qs_1, AXES, across)
    qs_2 = lax.ppermute(qs_2, AXES, across)
    q_e = lax.ppermute(q_e, AXES, within)
    gs_e = lax.ppermute(gs_e, AXES, within)
    acc = sds((rows, cols), F32)
    dqn, dk, dv = call(within_kernel, (low_s, acc, acc), [VM] * 8, (VM,) * 3, [], COSTS[1])(
        bias_e, q, k, v, g, kv_e, q_e, gs_e
    )
    dqm, dkn, dvn, dk, dv = call(across_kernel, (low_s,) * 3 + (part,) * 2, [VM] * 8, (VM,) * 5, [], COSTS[2])(
        bias_o, q, k, v, g, kv_o, dk, dv
    )
    done = sds((half, cut), BF16)
    dk1, dv1 = call(first_edge_kernel, (done, done), [VM] * 6, (VM,) * 2, [], COSTS[3])(bias_o, k, v, qs_1, dk, dv)
    rest = pltpu.VMEM((half, cols - cut), BF16)
    return call(
        last_kernel, (whole,) * 3, [VM] * 13, (HB,) * 3, [rest, rest, pltpu.SemaphoreType.DMA((8,))], COSTS[4]
    )(bias_o, k, v, qs_2, qs_1, dk, dv, dqn, dqm, dkn, dvn, dk1, dv1)


def solution(mesh):
    return jax.shard_map(
        body,
        mesh=mesh,
        in_specs=(P(AXES, None),) * 4 + (P(),),
        out_specs=(P(AXES, None),) * 3,
        check_vma=False,
    )
```

```python
import functools

import jax
import jax.numpy as jnp
from jax import lax
from jax.experimental import pallas as pl
from jax.experimental.pallas import tpu as pltpu
from jax.sharding import PartitionSpec as P

DH = 64
WIN = 64
PAIR = 2 * DH
STATS = 8
FAR_STATS = (0, 1, 2, 4, 5, 6)
MOVED = 16
COSTS = (1 << 28, 0, 1 << 31, 0, 1 << 27)
LAST = 2
SCALE = DH ** (-0.5)
NEG = -1e30
AXES = ("blk", "head")
F32 = jnp.float32
BF16 = jnp.bfloat16


def flat_index():
    return lax.axis_index("blk") * lax.axis_size("head") + lax.axis_index("head")


def recording_of(pos, len_ref):
    rec = jnp.where(pos < 0, -1, 0)
    end = jnp.int32(0)
    for r in range(len_ref.shape[0]):
        end = end + len_ref[r]
        rec = rec + jnp.where(pos >= end, 1, 0)
    return rec


def bias_of(key_first, query_first, keys, queries, lane_queries, len_ref):
    kpos = key_first + lax.broadcasted_iota(jnp.int32, (keys, 1), 0)
    qpos = query_first + lax.broadcasted_iota(jnp.int32, (1, queries), 1) % lane_queries
    near = jnp.abs(kpos - qpos) <= WIN
    same = recording_of(kpos, len_ref) == recording_of(qpos, len_ref)
    return jnp.where(near & same, 0.0, NEG).astype(F32)


def split_heads(pair):
    lane = lax.broadcasted_iota(jnp.int32, pair.shape, 1)
    zero = jnp.zeros_like(pair)
    return jnp.concatenate([jnp.where(lane < DH, pair, zero), jnp.where(lane < DH, zero, pair)], axis=0)


def nt(a, b):
    return lax.dot_general(a, b, (((1,), (1,)), ((), ())), preferred_element_type=F32)


def nn(a, b):
    return lax.dot_general(a, b, (((1,), (0,)), ((), ())), preferred_element_type=F32)


def tn(a, b):
    return lax.dot_general(a, b, (((0,), (0,)), ((), ())), preferred_element_type=F32)


def pieces(x):
    hi = x.astype(BF16).astype(F32)
    mid = (x - hi).astype(BF16).astype(F32)
    return [hi, mid, x - hi - mid]


def prep_kernel(len_hbm, k_hbm, v_hbm, k_ref, v_ref, kv_o, kv_e, own_bias, bias_o, bias_e, len_ref, sems):
    copies = [
        pltpu.make_async_copy(len_hbm, len_ref, sems.at[0]),
        pltpu.make_async_copy(k_hbm, k_ref, sems.at[1]),
        pltpu.make_async_copy(v_hbm, v_ref, sems.at[2]),
    ]
    for copy in copies:
        copy.start()
    rows = k_ref.shape[0]
    half = rows // 2
    me = flat_index()
    odd = lax.rem(me, 2)
    base = me * rows
    copies[0].wait()
    own_bias[...] = bias_of(base, base, rows, rows, rows, len_ref)
    for out, side in ((bias_o, odd), (bias_e, 1 - odd)):
        mine, other = base + side * half, base + jnp.where(side == 1, rows, -half)
        out[:rows, :] = bias_of(base, mine, rows, rows, half, len_ref)
        out[rows : rows + half, :] = bias_of(other, mine, half, rows, half, len_ref)
        out[rows + half :, :] = bias_of(mine, other, half, rows, half, len_ref)
    for n, ref in enumerate((k_ref, v_ref)):
        copies[n + 1].wait()
        kv_o[n * half : (n + 1) * half, :] = ref[pl.ds(pl.multiple_of(odd * half, half), half), :]
        size = half - n * MOVED
        kv_e[n * half : n * half + size, :] = ref[pl.ds(pl.multiple_of((1 - odd) * half, half), size), :]


def local_kernel(bias_ref, q_ref, k_ref, v_ref, g_ref, qs_1, qs_2, q_e, gs_e):
    rows, cols = q_ref.shape
    odd = lax.rem(flat_index(), 2)
    half = rows // 2
    first, other = pl.multiple_of(odd * half, half), pl.multiple_of((1 - odd) * half, half)
    cut = qs_1.shape[1]
    for out, cs in ((qs_1, slice(0, cut)), (qs_2, slice(cut, cols))):
        out[:half, :] = q_ref[pl.ds(first, half), cs] * BF16(SCALE)
        out[half:rows, :] = g_ref[pl.ds(first, half), cs]
    q_e[:half, :] = q_ref[pl.ds(other, half), :] * BF16(SCALE)
    q_e[half:, :] = v_ref[pl.ds(pl.multiple_of(other + half - MOVED, MOVED), MOVED), :]
    gs_e[:half, :] = g_ref[pl.ds(other, half), :]
    bias = bias_ref[...]
    bias = jnp.concatenate([bias, bias], axis=1)
    lane = lax.broadcasted_iota(jnp.int32, (1, rows), 1)
    far = []
    for p in range(cols // PAIR):
        cs = slice(p * PAIR, (p + 1) * PAIR)
        qq = split_heads(q_ref[:, cs]) * BF16(SCALE)
        gg = split_heads(g_ref[:, cs])
        s = nt(k_ref[:, cs], qq) + bias
        dp = nt(v_ref[:, cs], gg)
        m = jnp.max(s, axis=0, keepdims=True).astype(BF16).astype(F32)
        e = jnp.exp(s - m)
        l = jnp.sum(e, axis=0, keepdims=True)
        d = jnp.sum(e * dp, axis=0, keepdims=True)
        stat = jnp.concatenate([m] + pieces(l) + pieces(d) + [jnp.zeros_like(m)], axis=0)
        a, b = stat[:, :rows], stat[:, rows:]
        lo = jnp.where(lane < half, a, pltpu.roll(b, half, 1))
        hi = jnp.where(lane < half, pltpu.roll(a, half, 1), b)
        far.append(jnp.where(odd == 1, hi, lo))
        gs_e[half:, cs] = jnp.where(odd == 1, lo, hi).astype(BF16)
    for n, r in enumerate(FAR_STATS):
        block = jnp.concatenate([stat[r : r + 1] for stat in far], axis=0)
        qs_1[rows:, n * PAIR : (n + 1) * PAIR] = block.astype(BF16)


def side_rows(across, half):
    odd = lax.rem(flat_index(), 2)
    return pl.ds(pl.multiple_of((odd if across else 1 - odd) * half, half), half)


def own_half(rs, group, bias_ref, q_ref, k_ref, v_ref, g_ref, kn_ref, v_near, dq_ref, add):
    rows = k_ref.shape[0]
    half = rows // 2
    lane = lax.broadcasted_iota(jnp.int32, (half, PAIR), 1)
    near, far = bias_ref[:rows, :], bias_ref[rows : rows + half, :]
    scored = []
    for cs in group:
        qq = split_heads(q_ref[rs, cs]) * BF16(SCALE)
        gg = split_heads(g_ref[rs, cs])
        s = nt(k_ref[:, cs], qq), nt(kn_ref[:, cs], qq)
        dp = nt(v_ref[:, cs], gg), nt(v_near(cs), gg)
        scored.append((qq, gg, s, dp))
    graded = []
    for qq, gg, s, dp in scored:
        s = s[0] + near, s[1] + far
        m = jnp.maximum(jnp.max(s[0], axis=0, keepdims=True), jnp.max(s[1], axis=0, keepdims=True))
        e = [jnp.exp(x - m) for x in s]
        inv = 1.0 / (jnp.sum(e[0], axis=0, keepdims=True) + jnp.sum(e[1], axis=0, keepdims=True))
        prob = [x * inv for x in e]
        delta = jnp.sum(prob[0] * dp[0], axis=0, keepdims=True) + jnp.sum(prob[1] * dp[1], axis=0, keepdims=True)
        ds = [(x * (y - delta)).astype(BF16) for x, y in zip(prob, dp)]
        graded.append((qq, gg, prob[0].astype(BF16), ds))
    for cs, (qq, gg, prob, ds) in zip(group, graded):
        add(cs, nn(ds[0], qq), nn(prob, gg))
        dq2 = tn(ds[0], k_ref[:, cs]) + tn(ds[1], kn_ref[:, cs])
        dq_ref[:, cs] = (jnp.where(lane < DH, dq2[:half], dq2[half:]) * SCALE).astype(BF16)


def edge(rs, group, first, bias_ref, k_ref, v_ref, qn_ref, g_ref, stats, add):
    rows = k_ref.shape[0]
    half = rows // 2
    bias = bias_ref[rows + half :, :]
    scored = []
    for cs in group:
        ns = slice(cs.start - first, cs.stop - first)
        qq, gg = split_heads(qn_ref[:, ns]), split_heads(g_ref[:, ns])
        scored.append((qq, gg, nt(k_ref[rs, cs], qq), nt(v_ref[rs, cs], gg)))
    graded = []
    for cs, (qq, gg, s, dp) in zip(group, scored):
        m0, l0, d0 = stats(cs)
        s = s + bias
        m = jnp.maximum(m0, jnp.max(s, axis=0, keepdims=True))
        e = jnp.exp(s - m)
        a = jnp.exp(m0 - m)
        l = a * l0 + jnp.sum(e, axis=0, keepdims=True)
        d = a * d0 + jnp.sum(e * dp, axis=0, keepdims=True)
        inv = 1.0 / jnp.where(l > 0, l, 1.0)
        prob = e * inv
        graded.append((qq, gg, prob.astype(BF16), (prob * (dp - d * inv)).astype(BF16)))
    for cs, (qq, gg, prob, ds) in zip(group, graded):
        add(cs, nn(ds, qq), nn(prob, gg))


def pairs_of(first, end):
    return [slice(c, c + PAIR) for c in range(first, end, PAIR)]


def within_kernel(bias_ref, q_ref, k_ref, v_ref, g_ref, kv_ref, qn_ref, gs_ref, dq_ref, dk_ref, dv_ref):
    rows, cols = k_ref.shape
    half = rows // 2
    rs = side_rows(False, half)

    def put(cs, dk, dv):
        dk_ref[:, cs] = dk
        dv_ref[:, cs] = dv

    def add(cs, dk, dv):
        dk_ref[rs, cs] = dk_ref[rs, cs] + dk
        dv_ref[rs, cs] = dv_ref[rs, cs] + dv

    kn_ref = kv_ref.at[:half]

    def vn_ref(cs):
        return jnp.concatenate([kv_ref[half:, cs], qn_ref[half:, cs]], axis=0)

    own_half(rs, pairs_of(0, cols), bias_ref, q_ref, k_ref, v_ref, g_ref, kn_ref, vn_ref, dq_ref, put)

    def stats(cs):
        stat = gs_ref[half:, cs].astype(F32)
        return stat[0:1], stat[1:2] + stat[2:3] + stat[3:4], stat[4:5] + stat[5:6] + stat[6:7]

    edge(rs, pairs_of(0, cols), 0, bias_ref, k_ref, v_ref, qn_ref.at[:half], gs_ref.at[:half], stats, add)


def across_kernel(
    bias_ref, q_ref, k_ref, v_ref, g_ref, kv_ref, dka_ref, dva_ref, dqn, dq_out, dq_ref, dkn_ref, dvn_ref, dk_ref, dv_ref, sem
):
    rows, cols = k_ref.shape
    half = rows // 2
    copy = pltpu.make_async_copy(dqn, dq_out.at[side_rows(False, half)], sem)
    copy.start()
    odd = lax.rem(flat_index(), 2)

    def put(cs, dk, dv):
        for part, acc, mine, other in ((dk, dka_ref, dk_ref, dkn_ref), (dv, dva_ref, dv_ref, dvn_ref)):
            part = part + acc[:, cs]
            low, high = part[:half], part[half:]
            mine[:, cs] = jnp.where(odd == 1, high, low)
            other[:, cs] = jnp.where(odd == 1, low, high).astype(BF16)

    own_half(
        side_rows(True, half),
        pairs_of(0, cols),
        bias_ref,
        q_ref,
        k_ref,
        v_ref,
        g_ref,
        kv_ref.at[:half],
        lambda cs: kv_ref[half:, cs],
        dq_ref,
        put,
    )
    copy.wait()


def edge_into(first, bias_ref, k_ref, v_ref, qs_ref, st_ref, dka_ref, dva_ref, dk_ref, dv_ref):
    rows = k_ref.shape[0]
    half = rows // 2
    stat = st_ref[rows:, :].astype(F32)

    def stats(cs):
        p = cs.start // PAIR
        m, l1, l2, d1, d2, d3 = (stat[p : p + 1, n * PAIR : (n + 1) * PAIR] for n in range(len(FAR_STATS)))
        return m, l1 + l2, d1 + d2 + d3

    size = qs_ref.shape[1]

    def put(cs, dk, dv):
        to = slice(cs.start - first, cs.stop - first)
        dv_ref[:, to] = (dva_ref[:, cs] + dv).astype(BF16)
        dk_ref[:, to] = (dka_ref[:, cs] + dk).astype(BF16)

    edge(
        side_rows(True, half),
        pairs_of(first, first + size),
        first,
        bias_ref,
        k_ref,
        v_ref,
        qs_ref.at[:half],
        qs_ref.at[half:rows],
        stats,
        put,
    )


def first_edge_kernel(bias_ref, k_ref, v_ref, qs_ref, dka_ref, dva_ref, dk_ref, dv_ref):
    edge_into(0, bias_ref, k_ref, v_ref, qs_ref, qs_ref, dka_ref, dva_ref, dk_ref, dv_ref)


def last_kernel(
    bias_ref, k_ref, v_ref, qs_ref, st_ref, dka_ref, dva_ref, dqm, dkn, dvn, dk1, dv1, dq_in, dq_out, dk_out, dv_out, dk2, dv2, sems
):
    rows, cols = k_ref.shape
    half = rows // 2
    mine, other = side_rows(True, half), side_rows(False, half)
    first = cols - qs_ref.shape[1]
    early = [
        (dqm, dq_out.at[mine]),
        (dkn, dk_out.at[other]),
        (dvn, dv_out.at[other]),
        (dk1, dk_out.at[mine, :first]),
        (dv1, dv_out.at[mine, :first]),
    ]
    late = [(dk2, dk_out.at[mine, first:]), (dv2, dv_out.at[mine, first:])]
    copies = [pltpu.make_async_copy(a, b, sems.at[n]) for n, (a, b) in enumerate(early + late)]
    for copy in copies[: len(early)]:
        copy.start()
    edge_into(first, bias_ref, k_ref, v_ref, qs_ref, st_ref, dka_ref, dva_ref, dk2, dv2)
    for copy in copies[len(early) :]:
        copy.start()
    for copy in copies:
        copy.wait()


VM = pl.BlockSpec(memory_space=pltpu.VMEM)
HB = pl.BlockSpec(memory_space=pl.ANY)


def body(queries, key_vectors, value_vectors, grad_output, lengths):
    rows, cols = queries.shape
    half = rows // 2
    count = lax.axis_size("blk") * lax.axis_size("head")
    across = [(a, b) for i in range(1, count - 1, 2) for a, b in ((i, i + 1), (i + 1, i))]
    within = [(a, b) for i in range(0, count, 2) for a, b in ((i, i + 1), (i + 1, i))]

    sds = jax.ShapeDtypeStruct
    whole, part = sds((rows, cols), BF16), sds((half, cols), F32)
    low_s = sds((half, cols), BF16)
    sent_q, sent_g = sds((half + MOVED, cols), BF16), sds((half + STATS, cols), BF16)
    masks = sds((2 * rows, rows), F32)
    dma = pltpu.SemaphoreType.DMA((3,))

    def call(kernel, out_shape, in_specs, out_specs, scratch, flops, alias={}):
        return pl.pallas_call(
            kernel,
            out_shape=out_shape,
            in_specs=in_specs,
            out_specs=out_specs,
            scratch_shapes=scratch,
            input_output_aliases=alias,
            compiler_params=pltpu.CompilerParams(vmem_limit_bytes=20 << 20),
            cost_estimate=pl.CostEstimate(flops=flops, bytes_accessed=max(flops >> 10, 1), transcendentals=0),
        )

    k, v, kv_o, kv_e, own_bias, bias_o, bias_e = call(
        prep_kernel,
        (whole,) * 3 + (sds((rows - MOVED, cols), BF16), sds((rows, rows), F32), masks, masks),
        [HB] * 3,
        (VM,) * 7,
        [pltpu.SMEM(lengths.shape, jnp.int32), dma],
        1 << 20,
    )(*(pltpu.with_memory_space_constraint(x, pltpu.HBM) for x in (lengths, key_vectors, value_vectors)))
    kv_o = lax.ppermute(kv_o, AXES, across)
    kv_e = lax.ppermute(kv_e, AXES, within)
    q, g = queries, grad_output
    cut = cols - LAST * PAIR
    qs_1, qs_2, q_e, gs_e = call(
        local_kernel,
        (sds((rows + STATS, cut), BF16), sds((rows, cols - cut), BF16), sent_q, sent_g),
        [VM] * 5,
        (VM,) * 4,
        [],
        COSTS[0],
    )(own_bias, q, k, v, g)
    qs_1 = lax.ppermute(qs_1, AXES, across)
    qs_2 = lax.ppermute(qs_2, AXES, across)
    q_e = lax.ppermute(q_e, AXES, within)
    gs_e = lax.ppermute(gs_e, AXES, within)
    acc = sds((rows, cols), F32)
    dqn, dk, dv = call(within_kernel, (low_s, acc, acc), [VM] * 8, (VM,) * 3, [], COSTS[1])(
        bias_e, q, k, v, g, kv_e, q_e, gs_e
    )
    dq, dqm, dkn, dvn, dk, dv = call(
        across_kernel, (whole,) + (low_s,) * 3 + (part,) * 2, [VM] * 9, (HB,) + (VM,) * 5, [pltpu.SemaphoreType.DMA], COSTS[2]
    )(
        bias_o, q, k, v, g, kv_o, dk, dv, dqn
    )
    done = sds((half, cut), BF16)
    dk1, dv1 = call(first_edge_kernel, (done, done), [VM] * 6, (VM,) * 2, [], COSTS[3])(bias_o, k, v, qs_1, dk, dv)
    rest = pltpu.VMEM((half, cols - cut), BF16)
    return call(
        last_kernel, (whole,) * 3, [VM] * 12 + [HB], (HB,) * 3, [rest, rest, pltpu.SemaphoreType.DMA((7,))], COSTS[4], {12: 0}
    )(bias_o, k, v, qs_2, qs_1, dk, dv, dqm, dkn, dvn, dk1, dv1, dq)


def solution(mesh):
    return jax.shard_map(
        body,
        mesh=mesh,
        in_specs=(P(AXES, None),) * 4 + (P(),),
        out_specs=(P(AXES, None),) * 3,
        check_vma=False,
    )
```
